256 devices in a mesh: pole: 16 (over z, core), row: 4 (over y), col: 4 (over x).
Axes of the slice: x: 4, y: 4, z: 8, core: 2. Of those that a mesh axis runs over, the one named last changes fastest.
Arguments:
- inverse_trail: bfloat16 [16, 1024, 2, 1024], P('pole', 'row', None, 'col'), may hold values from -6 to 6
- lower_t: bfloat16 [16, 2048, 2, 1024], P('pole', 'col', None, 'row'), may hold values from -0.125 to 0.125
- diag_inverse: bfloat16 [16, 2048, 2, 2048], P('pole', 'row', None, 'col'), may hold values from -6 to 6
- pole_weight: float32 [256, 2], replicated, may hold values from -4 to 4
- pole_slot: int32 [16], P('pole'), may hold values from 0 to 255
- pair_row: int32 [8192], replicated, may hold values from 0 to 383, as said below
- pair_col: int32 [8192], replicated, may hold values from 0 to 255, as said below
- projector: bfloat16 [8192, 64], P('pole'), may hold values from -6 to 6
Outputs:
- diag_block: bfloat16 [16, 2048, 2, 2048], P('pole', 'row', None, 'col')
- pair_density: float32 [8192, 128], P('pole')
The draws below stay inside these ranges and needn't reach their ends.
Inputs may be any that keep to these rules, and one draw needn't show every extreme that they name: `pair_row`: pairs come in aligned blocks of 512, one block for each index of pole. A pair's grid cell is (a // (256 // size of row), b // (256 // size of col)) for a supernode row atom a and column atom b, and (b // (256 // size of row), (a - 256) // (128 // size of col)) otherwise. In every block at most 64 pairs share one grid cell, and some cell holds exactly 64. `pair_col`: drawn together with pair_row.
All inputs are finite; a program needn't handle non-finite values.
Results may differ from the reference program's by a relative error of at most 0.0038.
Values may be sent and summed in bfloat16 or wider, within the bound.
No kernel may reach another device: no remote copies, remote signals or barrier semaphores. Data moves between devices by JAX's collectives and lax.ppermute only.
A program may use at most 64 MiB of HBM per device.

```python
import jax
import jax.numpy as jnp
from jax import lax

K = 2048
M = 1024
B = 8
WTAB = 256
PAIR_DEV = 512
POLES = 16
KA = 256
MA = 128
NPAIR = 8192
N_POLE = 16
N_ROW = 4
N_COL = 4


def pair_layout(key):
    base = jax.random.fold_in(key, 7711)
    cells = N_ROW * N_COL
    most = 2 * PAIR_DEV // cells
    keys = jax.random.split(base, 7)
    first = jax.random.randint(keys[0], (N_POLE,), 0, cells)
    block_keys = jax.random.split(keys[1], N_POLE)
    others = jax.vmap(lambda k: jax.random.permutation(k, cells - 1))(block_keys)
    place = jnp.arange(PAIR_DEV, dtype=jnp.int32)
    spread = jnp.take_along_axis(others, jnp.broadcast_to(jnp.maximum(place - most, 0) % (cells - 1), (N_POLE, PAIR_DEV)), axis=1)
    spread = (first[:, None] + 1 + spread) % cells
    cell = jnp.where(place[None, :] < most, first[:, None], spread)
    order_keys = jax.random.split(keys[2], N_POLE)
    orders = jax.vmap(lambda k: jax.random.permutation(k, PAIR_DEV))(order_keys)
    cell = jnp.take_along_axis(cell, orders, axis=1).reshape(NPAIR)
    grid_row = cell // N_COL
    grid_col = cell % N_COL
    row_atoms = KA // N_ROW
    col_atoms = KA // N_COL
    trail_atoms = MA // N_COL
    is_super = jax.random.randint(keys[3], (NPAIR,), 0, 2) == 1
    first_pick = jax.random.randint(keys[4], (NPAIR,), 0, 1 << 20)
    second_pick = jax.random.randint(keys[5], (NPAIR,), 0, 1 << 20)
    other_pick = jax.random.randint(keys[6], (NPAIR,), 0, 1 << 20)
    low_pick = jnp.minimum(first_pick, second_pick)
    super_row = grid_row * row_atoms + low_pick % row_atoms
    super_col = grid_col * col_atoms + other_pick % col_atoms
    trail_row = KA + grid_col * trail_atoms + low_pick % trail_atoms
    trail_col = grid_row * row_atoms + other_pick % row_atoms
    rows = jnp.where(is_super, super_row, trail_row).astype(jnp.int32)
    columns = jnp.where(is_super, super_col, trail_col).astype(jnp.int32)
    return (rows, columns)


def draw_pair_row(key, part):
    return pair_layout(key)[0]


def draw_pair_col(key, part):
    return pair_layout(key)[1]


def with_ends(array, key, low, high):
    longest = array.shape.index(max(array.shape))
    spots = []
    for shift in (0, 1):
        where = [jax.random.randint(jax.random.fold_in(key, axis), (), 0, length) for axis, length in enumerate(array.shape)]
        where[longest] = (where[longest] + shift) % array.shape[longest]
        spots.append(tuple(where))
    return array.at[spots[0]].set(low).at[spots[1]].set(high)


def level_of(own_key, shape, cuts, low, largest):
    level = 1.0
    for axis_at, shards_of in cuts:
        heights = jax.random.uniform(jax.random.fold_in(jax.random.fold_in(own_key, 6), axis_at), (shards_of,), jnp.float32, low / len(cuts), largest / len(cuts))
        level = level * jnp.repeat(jnp.exp(heights), shape[axis_at] // shards_of).reshape((-1,) + (1,) * (len(shape) - 1 - axis_at))
    return level


def scatter_about(rng, extent, scale, reach, cuts=(), held_as=jnp.bfloat16):
    values = scale * jax.random.normal(rng, extent, jnp.float32)
    if cuts:
        values = values * level_of(rng, extent, cuts, -0.22, 0.18)
    return jnp.clip(values, -reach, reach).astype(held_as)


def setup_inputs(seed: int = 0) -> dict:
    streams_of = jax.random.split(jax.random.key(seed), 9)
    inverse_trail = scatter_about(streams_of[0], (POLES, M, 2, M), 1.0, 6.0, ((0, 16), (1, 4), (3, 4)))
    lower_t = scatter_about(streams_of[1], (POLES, K, 2, M), (2 * M) ** -0.5, 0.125, ((0, 16), (1, 4), (3, 4)))
    diag_inverse = scatter_about(streams_of[2], (POLES, K, 2, K), 1.0, 6.0, ((0, 16), (1, 4), (3, 4)))
    pole_weight = scatter_about(streams_of[3], (WTAB, 2), 1.0, 4.0, (), jnp.float32)
    pole_slot = with_ends(jax.random.randint(streams_of[4], (POLES,), 0, WTAB), jax.random.fold_in(streams_of[4], 1), 0, WTAB - 1).astype(jnp.int32)
    pair_row = draw_pair_row(jax.random.fold_in(streams_of[8], 71), 0)
    pair_col = draw_pair_col(jax.random.fold_in(streams_of[8], 71), 0)
    projector = scatter_about(streams_of[7], (NPAIR, B * B), 1.0, 6.0, ((0, 16),))
    return {"inverse_trail": inverse_trail, "lower_t": lower_t, "diag_inverse": diag_inverse, "pole_weight": pole_weight, "pole_slot": pole_slot, "pair_row": pair_row, "pair_col": pair_col, "projector": projector}


def cproduct(left_side, right_side):
    real_a = left_side[:, 0, :]
    imag_a = left_side[:, 1, :]
    real_b = right_side[:, 0, :]
    imag_b = right_side[:, 1, :]
    real_out = jnp.dot(real_a, real_b, preferred_element_type=jnp.float32) - jnp.dot(imag_a, imag_b, preferred_element_type=jnp.float32)
    imag_out = jnp.dot(real_a, imag_b, preferred_element_type=jnp.float32) + jnp.dot(imag_a, real_b, preferred_element_type=jnp.float32)
    return jnp.stack([real_out, imag_out], axis=1)


def reference(inverse_trail, lower_t, diag_inverse, pole_weight, pole_slot, pair_row, pair_col, projector):
    weights = pole_weight[pole_slot]
    in_super = pair_row < KA
    super_index = jnp.minimum(pair_row, KA - 1)
    trail_index = jnp.clip(pair_row - KA, 0, MA - 1)

    def one_pole(packed):
        trail, lower, inverse, weight = packed
        coupling = (-cproduct(lower, trail)).astype(jnp.bfloat16)
        lower_swap = jnp.transpose(lower, (2, 1, 0))
        block = (inverse.astype(jnp.float32) - cproduct(coupling, lower_swap)).astype(jnp.bfloat16)
        table_super = block.reshape(KA, B, 2, KA, B).transpose(0, 3, 2, 1, 4)
        table_trail = coupling.reshape(KA, B, 2, MA, B).transpose(3, 0, 2, 4, 1)
        from_super = table_super[super_index, pair_col]
        from_trail = table_trail[trail_index, pair_col]
        chosen = jnp.where(in_super[:, None, None, None], from_super, from_trail)
        chosen = chosen.astype(jnp.float32).reshape(NPAIR, 2, B * B)
        real_part = weight[0] * chosen[:, 0] - weight[1] * chosen[:, 1]
        imag_part = weight[0] * chosen[:, 1] + weight[1] * chosen[:, 0]
        return block, jnp.stack([real_part, imag_part], axis=1)

    blocks, weighted = lax.map(one_pole, (inverse_trail, lower_t, diag_inverse, weights))
    summed = jnp.sum(weighted, axis=0)
    density = summed * projector.astype(jnp.float32)[:, None, :]
    return blocks, density.reshape(NPAIR, 2 * B * B)
```

```python
import jax
import jax.numpy as jnp
from jax import lax
from jax.experimental import pallas as pl
from jax.experimental.pallas import tpu as pltpu
from jax.sharding import Mesh
from jax.sharding import PartitionSpec as P

B = 8
KA = 256
POLE = ("pole_0", "pole_1")
ROWS = 4
COLS = 4
SLOTS = 64
MIB = 1 << 20


def ring(shift, peers):
    return [(i, (i + shift) % peers) for i in range(peers)]


def to_process_rows(shift):
    return [
        (k * COLS + x, x * COLS + (k + shift) % COLS) for k in range(ROWS) for x in range(COLS)
    ]


def atoms_apart(raw):
    rows, _, columns = raw.shape
    return raw.reshape(rows // B, B, 2, columns).transpose(0, 2, 1, 3).reshape(2 * rows, columns)


def whole(shape):
    return pl.BlockSpec(shape, lambda *_: (0,) * len(shape))


def contract(left, right, dim):
    return lax.dot_general(
        left, right, (((1,), (dim,)), ((), ())), preferred_element_type=jnp.float32
    )


def coupling_kernel(base_ref, l0, l1, l2, l3, t_ref, c_ref, ct_ref):
    tile = c_ref.shape[0]
    columns = c_ref.shape[1]
    real = imag = None
    for d, left in enumerate((l0, l1, l2, l3)):
        e = (base_ref[0] + d) % ROWS
        u = contract(left[...], t_ref[e, 0], 0)
        v = contract(left[...], t_ref[e, 1], 0)
        real = u if real is None else real + u
        imag = v if imag is None else imag + v
    u = real.reshape(tile // 16, 2, 8, columns)
    v = imag.reshape(tile // 16, 2, 8, columns)
    re = v[:, 1] - u[:, 0]
    im = -(u[:, 1] + v[:, 0])
    c_ref[...] = jnp.stack([re, im], axis=1).reshape(tile, columns).astype(jnp.bfloat16)
    re_t = re.reshape(tile // 2, columns).T.reshape(columns // 8, 8, tile // 2)
    im_t = im.reshape(tile // 2, columns).T.reshape(columns // 8, 8, tile // 2)
    ct_ref[...] = (
        jnp.stack([re_t, im_t], axis=1).reshape(2 * columns, tile // 2).astype(jnp.bfloat16)
    )


def coupling_call(base, lefts, trail):
    rows, inner = lefts[0].shape
    columns = trail.shape[3]
    tile = 256
    left_spec = pl.BlockSpec((tile, inner), lambda i, *_: (i, 0))
    return pl.pallas_call(
        coupling_kernel,
        out_shape=(
            jax.ShapeDtypeStruct((rows, columns), jnp.bfloat16),
            jax.ShapeDtypeStruct((2 * columns, rows // 2), jnp.bfloat16),
        ),
        grid_spec=pltpu.PrefetchScalarGridSpec(
            num_scalar_prefetch=1,
            grid=(rows // tile,),
            in_specs=[left_spec] * 4 + [whole(trail.shape)],
            out_specs=(
                pl.BlockSpec((tile, columns), lambda i, *_: (i, 0)),
                pl.BlockSpec((2 * columns, tile // 2), lambda i, *_: (0, i)),
            ),
        ),
        cost_estimate=pl.CostEstimate(
            flops=2 * rows * inner * 8 * columns, bytes_accessed=6 << 20, transcendentals=0
        ),
        name="coupling",
    )(base, *lefts, trail)


def block_kernel(
    base_ref, codes_ref, c0, c1, c2, c3, l_ref, diag_ref, ct_ref, mask_ref, out_ref, pairs_ref,
    table, lanes, spread, keep, fold,
):
    rows, columns = diag_ref.shape
    step = pl.program_id(0)
    tile = c0.shape[0]

    @pl.when(step == 0)
    def _():
        table[rows : rows + ct_ref.shape[0], :] = ct_ref[...]
        lane = lax.broadcasted_iota(jnp.int32, (128, 128), 1)
        row = lax.broadcasted_iota(jnp.int32, (128, 128), 0)
        spread[...] = jnp.where(row % 8 == lane % 8, 1.0, 0.0).astype(jnp.bfloat16)
        row = lax.broadcasted_iota(jnp.int32, (16, 128), 0)
        lane = lax.broadcasted_iota(jnp.int32, (16, 128), 1)
        keep[...] = jnp.where(lane // 8 == row, 1.0, 0.0)
        row = lax.broadcasted_iota(jnp.int32, fold.shape, 0)
        lane = lax.broadcasted_iota(jnp.int32, fold.shape, 1)
        fold[...] = jnp.where(lane // 16 == row, 1.0, 0.0).astype(jnp.bfloat16)

    real = imag = None
    for d, left in enumerate((c0, c1, c2, c3)):
        e = (base_ref[0] + d) % ROWS
        u = contract(left[...], l_ref[e, 0], 1)
        v = contract(left[...], l_ref[e, 1], 1)
        real = u if real is None else real + u
        imag = v if imag is None else imag + v
    u = real.reshape(tile // 16, 2, 8, columns)
    v = imag.reshape(tile // 16, 2, 8, columns)
    start = pl.multiple_of(step * tile, tile)
    diag = diag_ref[pl.ds(start, tile), :].astype(jnp.float32).reshape(tile // 16, 2, 8, columns)
    re = diag[:, 0] - (u[:, 0] - v[:, 1])
    im = diag[:, 1] - (u[:, 1] + v[:, 0])
    block = jnp.stack([re, im], axis=1).reshape(tile, columns).astype(jnp.bfloat16)
    out_ref[...] = block
    table[pl.ds(start, tile), :] = block

    @pl.when(step == pl.num_programs(0) - 1)
    def _():
        @pl.loop(0, pairs_ref.shape[0] // SLOTS)
        def _(owner):
            first = owner * SLOTS
            for s in range(SLOTS):
                code = codes_ref[first + s]
                at = pl.multiple_of((code >> 6) * 16, 16)
                across = pl.multiple_of(((code >> 4) & 3) * 128, 128)
                found = table[pl.ds(at, 16), pl.ds(across, 128)]
                lanes[s * 16 : s * 16 + 16, :] = found * mask_ref[code & 15]
            wide = contract(lanes[...], spread[...], 0).reshape(SLOTS, 16, 128)
            wide = (wide * keep[...][None]).reshape(SLOTS * 16, 128).astype(jnp.bfloat16)
            pairs_ref[pl.ds(pl.multiple_of(first, SLOTS), SLOTS), :] = contract(
                fold[...], wide, 0
            ).astype(jnp.bfloat16)


def block_call(base, codes, couplings, lower, diag, coupling_t, masks):
    rows, columns = diag.shape
    inner = couplings[0].shape[1]
    slots = codes.shape[0]
    tile = 256
    return pl.pallas_call(
        block_kernel,
        out_shape=(
            jax.ShapeDtypeStruct((rows, columns), jnp.bfloat16),
            jax.ShapeDtypeStruct((slots, 2 * B * B), jnp.bfloat16),
        ),
        grid_spec=pltpu.PrefetchScalarGridSpec(
            num_scalar_prefetch=2,
            grid=(rows // tile,),
            in_specs=[pl.BlockSpec((tile, inner), lambda i, *_: (i, 0))] * 4
            + [whole(lower.shape), whole(diag.shape), whole(coupling_t.shape), whole(masks.shape)],
            out_specs=(
                pl.BlockSpec((tile, columns), lambda i, *_: (i, 0)),
                whole((slots, 2 * B * B)),
            ),
            scratch_shapes=[
                pltpu.VMEM((rows + coupling_t.shape[0], columns), jnp.bfloat16),
                pltpu.VMEM((SLOTS * 16, 128), jnp.bfloat16),
                pltpu.VMEM((128, 128), jnp.bfloat16),
                pltpu.VMEM((16, 128), jnp.float32),
                pltpu.VMEM((SLOTS, SLOTS * 16), jnp.bfloat16),
            ],
        ),
        compiler_params=pltpu.CompilerParams(vmem_limit_bytes=40 * MIB),
        cost_estimate=pl.CostEstimate(
            flops=2 * rows * inner * 8 * columns, bytes_accessed=12 << 20, transcendentals=0
        ),
        name="block_and_pairs",
    )(base, codes, *couplings, lower, diag, coupling_t, masks)


def pole_sum_kernel(weight_ref, parts_ref, out_ref):
    straight = crossed = None
    for p in range(parts_ref.shape[0]):
        part = parts_ref[p].astype(jnp.float32)
        a = weight_ref[p, 0] * part
        b = weight_ref[p, 1] * part
        straight = a if straight is None else straight + a
        crossed = b if crossed is None else crossed + b
    half = B * B
    lane = lax.broadcasted_iota(jnp.int32, crossed.shape, 1)
    crossed = pltpu.roll(crossed, half, 1)
    out_ref[...] = straight + jnp.where(lane < half, -crossed, crossed)


def pole_sum_call(weights, parts):
    return pl.pallas_call(
        pole_sum_kernel,
        out_shape=jax.ShapeDtypeStruct(parts.shape[1:], jnp.float32),
        in_specs=[pl.BlockSpec(memory_space=pltpu.SMEM), pl.BlockSpec(memory_space=pltpu.VMEM)],
        out_specs=pl.BlockSpec(memory_space=pltpu.VMEM),
        name="pole_sum",
    )(weights, parts)


def density_kernel(index_ref, sums_ref, projector_ref, out_ref):
    @pl.loop(0, out_ref.shape[0] // 16)
    def _(group):
        first = pl.multiple_of(group * 16, 16)
        for s in range(16):
            q = first + s
            out_ref[pl.ds(q, 1), :] = sums_ref[pl.ds(index_ref[q], 1), :]
        here = pl.ds(first, 16)
        out_ref[here, :] = out_ref[here, :] * projector_ref[here, :]


def density_call(index, sums, projector):
    return pl.pallas_call(
        density_kernel,
        out_shape=jax.ShapeDtypeStruct(projector.shape, jnp.float32),
        in_specs=[pl.BlockSpec(memory_space=pltpu.SMEM)]
        + [pl.BlockSpec(memory_space=pltpu.VMEM)] * 2,
        out_specs=pl.BlockSpec(memory_space=pltpu.VMEM),
        name="density",
    )(index, sums, projector)


def pair_tables(pair_row, pair_col, row, col, pole, owners):
    row_atoms, col_atoms, trail_atoms = KA // ROWS, KA // COLS, 128 // COLS
    a = pair_row.reshape(owners, -1)
    b = pair_col.reshape(owners, -1)
    in_super = a < KA
    trail = a - KA
    cell = jnp.where(
        in_super,
        (a // row_atoms) * COLS + b // col_atoms,
        (b // row_atoms) * COLS + trail // trail_atoms,
    )
    code = jnp.where(
        in_super,
        (a % row_atoms) * col_atoms + b % col_atoms,
        (row_atoms + trail % trail_atoms) * col_atoms + b % row_atoms,
    )
    pairs = a.shape[1]
    place = jnp.arange(pairs, dtype=jnp.int32)
    earlier = place[:, None] < place[None, :]
    mine = cell == row * COLS + col
    rank = jnp.dot(
        mine.astype(jnp.bfloat16),
        earlier.astype(jnp.bfloat16),
        preferred_element_type=jnp.float32,
    ).astype(jnp.int32)
    slot = jnp.where(mine, rank, -1)
    hit = slot[:, None, :] == jnp.arange(SLOTS, dtype=jnp.int32)[None, :, None]
    codes = jnp.sum(jnp.where(hit, code[:, None, :], 0), axis=2).reshape(owners * SLOTS)
    own_cell = lax.dynamic_index_in_dim(cell, pole, 0, keepdims=False)
    same = (own_cell[:, None] == own_cell[None, :]) & earlier
    index = own_cell * SLOTS + jnp.sum(same.astype(jnp.int32), axis=0)
    return codes, index


def local(
    inverse_trail, lower_t, diag_inverse, pole_weight, pole_slot, pair_row, pair_col, projector
):
    row = lax.axis_index("row")
    col = lax.axis_index("col")
    pole = lax.axis_index(POLE)
    poles = lax.axis_size(POLE)
    base = ((row - col + COLS) % COLS).astype(jnp.int32).reshape(1)

    trail = inverse_trail[0]
    lower = lower_t[0]

    trails = [trail] + [lax.ppermute(trail, "row", ring(e, ROWS)) for e in range(1, ROWS)]
    lefts = [lax.ppermute(lower, ("row", "col"), to_process_rows(d)) for d in range(COLS)]

    slots = lax.all_gather(pole_slot, POLE, axis=0, tiled=True)
    chosen = slots[:, None] == jnp.arange(pole_weight.shape[0], dtype=jnp.int32)[None, :]
    weights = jnp.sum(jnp.where(chosen[:, :, None], pole_weight[None], 0.0), axis=1)
    codes, index = pair_tables(pair_row, pair_col, row, col, pole, poles)
    diag = atoms_apart(diag_inverse[0])
    wide_projector = jnp.concatenate([projector, projector], axis=1).astype(jnp.float32)
    masks = (
        jnp.arange(16, dtype=jnp.int32)[:, None, None]
        == jnp.broadcast_to(jnp.arange(128, dtype=jnp.int32) // B, (16, 128))[None]
    ).astype(jnp.bfloat16)

    trail_all = jnp.stack([t.transpose(1, 0, 2) for t in trails])
    coupling, coupling_t = coupling_call(base, [atoms_apart(left) for left in lefts], trail_all)

    lower_late, _ = lax.optimization_barrier((lower, lefts))
    couplings = [coupling] + [
        lax.ppermute(coupling, "col", ring(d, COLS)) for d in range(1, COLS)
    ]
    lowers = [lower] + [lax.ppermute(lower_late, "row", ring(e, ROWS)) for e in range(1, ROWS)]
    lower_all = jnp.stack([x.transpose(1, 0, 2) for x in lowers])

    block, pairs = block_call(base, codes, couplings, lower_all, diag, coupling_t, masks)
    super_rows = block.shape[0] // 2
    out = (
        block.reshape(super_rows // B, 2, B, block.shape[1])
        .transpose(0, 2, 1, 3)
        .reshape(1, super_rows, 2, block.shape[1])
    )

    parts = lax.all_to_all(pairs.reshape(poles, SLOTS, 2 * B * B), POLE, 0, 0, tiled=True)
    summed = pole_sum_call(weights, parts)
    cells = ROWS * COLS
    everywhere = lax.all_to_all(
        jnp.broadcast_to(summed[None], (cells, *summed.shape)), ("row", "col"), 0, 0, tiled=True
    )
    density = density_call(index, everywhere.reshape(cells * SLOTS, 2 * B * B), wide_projector)
    return (out, density)


def solution(mesh):
    split = Mesh(
        mesh.devices.reshape(8, 2, mesh.shape["row"], mesh.shape["col"]),
        ("pole_0", "pole_1", "row", "col"),
    )
    in_specs = (
        P(POLE, "row", None, "col"),
        P(POLE, "col", None, "row"),
        P(POLE, "row", None, "col"),
        P(),
        P(POLE),
        P(),
        P(),
        P(POLE, None),
    )
    out_specs = (P(POLE, "row", None, "col"), P(POLE, None))
    return jax.shard_map(local, mesh=split, in_specs=in_specs, out_specs=out_specs, check_vma=False)
```

```python
import jax
import jax.numpy as jnp
from jax import lax
from jax.experimental import pallas as pl
from jax.experimental.pallas import tpu as pltpu
from jax.sharding import Mesh
from jax.sharding import PartitionSpec as P

B = 8
KA = 256
POLE = ("pole_0", "pole_1")
ROWS = 4
COLS = 4
SLOTS = 64
MIB = 1 << 20


def ring(shift, peers):
    return [(i, (i + shift) % peers) for i in range(peers)]


def to_process_rows(shift):
    return [
        (k * COLS + x, x * COLS + (k + shift) % COLS) for k in range(ROWS) for x in range(COLS)
    ]


def parts_apart(raw):
    return raw.transpose(1, 0, 2)


def whole(shape):
    return pl.BlockSpec(shape, lambda *_: (0,) * len(shape))


def product(left, right, dim):
    return lax.dot_general(
        left, right, (((1,), (dim,)), ((), ())), preferred_element_type=jnp.float32
    )


def complex_product(lefts, rights, dim, order):
    left = jnp.concatenate([x[...].reshape(-1, x.shape[2]) for x in lefts], axis=1)
    real = jnp.concatenate([rights[e][0] for e in order], axis=dim)
    imag = jnp.concatenate([rights[e][1] for e in order], axis=dim)
    half = left.shape[0] // 2
    u = product(left, real, dim)
    v = product(left, imag, dim)
    return u[:half] - v[half:], u[half:] + v[:half]


def by_atom(re, im):
    rows, columns = re.shape
    pair = [x.reshape(rows // B, B, columns) for x in (re, im)]
    return jnp.stack(pair, axis=1).reshape(2 * rows, columns).astype(jnp.bfloat16)


def coupling_kernel(base_ref, l0, l1, l2, l3, t0, t1, t2, t3, c_ref, ct_ref):
    def run(order):
        re, im = complex_product((l0, l1, l2, l3), (t0, t1, t2, t3), 0, order)
        c_ref[0] = (-re).astype(jnp.bfloat16)
        c_ref[1] = (-im).astype(jnp.bfloat16)
        ct_ref[...] = by_atom((-re).T, (-im).T)

    for base in range(ROWS):

        @pl.when(base_ref[0] == base)
        def _():
            run([(base + d) % ROWS for d in range(ROWS)])


def coupling_call(base, lefts, trails):
    _, rows, inner = lefts[0].shape
    columns = trails[0].shape[2]
    tile = 256
    left_spec = pl.BlockSpec((2, tile, inner), lambda i, *_: (0, i, 0))
    return pl.pallas_call(
        coupling_kernel,
        out_shape=(
            jax.ShapeDtypeStruct((2, rows, columns), jnp.bfloat16),
            jax.ShapeDtypeStruct((2 * columns, rows), jnp.bfloat16),
        ),
        grid_spec=pltpu.PrefetchScalarGridSpec(
            num_scalar_prefetch=1,
            grid=(rows // tile,),
            in_specs=[left_spec] * 4 + [whole(trails[0].shape)] * 4,
            out_specs=(
                pl.BlockSpec((2, tile, columns), lambda i, *_: (0, i, 0)),
                pl.BlockSpec((2 * columns, tile), lambda i, *_: (0, i)),
            ),
        ),
        compiler_params=pltpu.CompilerParams(vmem_limit_bytes=24 * MIB),
        cost_estimate=pl.CostEstimate(
            flops=2 * rows * inner * 16 * columns, bytes_accessed=6 << 20, transcendentals=0
        ),
        name="coupling",
    )(base, *lefts, *trails)


def take_pairs(codes_ref, mask_ref, pairs_ref, table, lanes, spread, keep, fold):
    @pl.loop(0, pairs_ref.shape[0])
    def _(owner):
        for s in range(SLOTS):
            code = codes_ref[owner * SLOTS + s]
            found = table[pl.ds(pl.multiple_of(code & ~15, 16), 16), :]
            lanes[s * 16 : s * 16 + 16, :] = found * mask_ref[code & 15]
        wide = product(lanes[...], spread[...], 0).reshape(SLOTS, 2, 8, 2 * B * B)
        wide = wide * keep[...][None]
        wide = (wide[:, 0] + wide[:, 1]).reshape(SLOTS * 8, 2 * B * B).astype(jnp.bfloat16)
        pairs_ref[owner, :SLOTS, :] = product(fold[...], wide, 0).astype(jnp.bfloat16)


def block_kernel(
    base_ref, slot_ref, codes_ref, c0, c1, c2, c3, l0, l1, l2, l3, diag_ref, ct_ref, mask_ref,
    out_ref, pairs_ref, table, lanes, spread, keep, fold,
):
    step = pl.program_id(0)
    last = pl.num_programs(0) - 1
    tile = out_ref.shape[1]
    per_tile = table.shape[0] // 4
    super_rows = per_tile - ct_ref.shape[0]

    @pl.when(step == 0)
    def _():
        for t in range(4):
            first = t * per_tile + super_rows
            table[first : first + ct_ref.shape[0], :] = ct_ref[:, t * 128 : t * 128 + 128]
        lane = lax.broadcasted_iota(jnp.int32, (128, 128), 1)
        row = lax.broadcasted_iota(jnp.int32, (128, 128), 0)
        spread[...] = jnp.where(row % 8 == lane % 8, 1.0, 0.0).astype(jnp.bfloat16)
        part = lax.broadcasted_iota(jnp.int32, (2, 8, 128), 0)
        row = lax.broadcasted_iota(jnp.int32, (2, 8, 128), 1)
        lane = lax.broadcasted_iota(jnp.int32, (2, 8, 128), 2)
        keep[...] = jnp.where(lane // 8 == part * 8 + row, 1.0, 0.0)
        row = lax.broadcasted_iota(jnp.int32, fold.shape, 0)
        lane = lax.broadcasted_iota(jnp.int32, fold.shape, 1)
        fold[...] = jnp.where(lane // 8 == row, 1.0, 0.0).astype(jnp.bfloat16)
        slot = jnp.full((16, 128), slot_ref[0], jnp.int32).astype(jnp.float32)
        for owner in range(pairs_ref.shape[0]):
            pairs_ref[owner, SLOTS:, :] = slot.astype(jnp.bfloat16)

    def run(order):
        re, im = complex_product((c0, c1, c2, c3), (l0, l1, l2, l3), 1, order)
        re = diag_ref[0].astype(jnp.float32) - re
        im = diag_ref[1].astype(jnp.float32) - im
        out_ref[0] = re.astype(jnp.bfloat16)
        out_ref[1] = im.astype(jnp.bfloat16)
        rows = by_atom(re, im)
        for t in range(4):
            first = pl.multiple_of(t * per_tile + step * 2 * tile, 2 * tile)
            table[pl.ds(first, 2 * tile), :] = rows[:, t * 128 : t * 128 + 128]

    for base in range(ROWS):

        @pl.when(base_ref[0] == base)
        def _():
            run([(base + d) % ROWS for d in range(ROWS)])

    @pl.when(step == last)
    def _():
        take_pairs(codes_ref, mask_ref, pairs_ref, table, lanes, spread, keep, fold)


def block_call(base, slot, codes, couplings, lowers, diag, coupling_t, masks):
    _, rows, columns = diag.shape
    inner = couplings[0].shape[2]
    owners = codes.shape[0] // SLOTS
    tile = 256
    row_spec = lambda last: pl.BlockSpec((2, tile, last), lambda i, *_: (0, i, 0))
    return pl.pallas_call(
        block_kernel,
        out_shape=(
            jax.ShapeDtypeStruct((2, rows, columns), jnp.bfloat16),
            jax.ShapeDtypeStruct((owners, SLOTS + 16, 2 * B * B), jnp.bfloat16),
        ),
        grid_spec=pltpu.PrefetchScalarGridSpec(
            num_scalar_prefetch=3,
            grid=(rows // tile,),
            in_specs=[row_spec(inner)] * 4
            + [whole(lowers[0].shape)] * 4
            + [row_spec(columns), whole(coupling_t.shape), whole(masks.shape)],
            out_specs=(row_spec(columns), whole((owners, SLOTS + 16, 2 * B * B))),
            scratch_shapes=[
                pltpu.VMEM((4 * (2 * rows + coupling_t.shape[0]), 128), jnp.bfloat16),
                pltpu.VMEM((SLOTS * 16, 128), jnp.bfloat16),
                pltpu.VMEM((128, 128), jnp.bfloat16),
                pltpu.VMEM((2, 8, 128), jnp.float32),
                pltpu.VMEM((SLOTS, SLOTS * 8), jnp.bfloat16),
            ],
        ),
        compiler_params=pltpu.CompilerParams(vmem_limit_bytes=40 * MIB),
        cost_estimate=pl.CostEstimate(
            flops=2 * rows * inner * 16 * columns, bytes_accessed=12 << 20, transcendentals=0
        ),
        name="block_and_pairs",
    )(base, slot, codes, *couplings, *lowers, diag, coupling_t, masks)


def pole_sum_kernel(weight_ref, parts_ref, out_ref):
    lane = lax.broadcasted_iota(jnp.int32, (1, 128), 1).astype(jnp.float32)
    straight = crossed = None
    for p in range(parts_ref.shape[0]):
        part = parts_ref[p, :SLOTS, :].astype(jnp.float32)
        slot = parts_ref[p, SLOTS:, :].astype(jnp.float32)[:1]
        weight = []
        for c in range(2):
            found = jnp.where(slot == lane, weight_ref[c : c + 1, :128], 0.0) + jnp.where(
                slot == lane + 128.0, weight_ref[c : c + 1, 128:], 0.0
            )
            weight.append(jnp.sum(found, axis=1, keepdims=True))
        a = weight[0] * part
        b = weight[1] * part
        straight = a if straight is None else straight + a
        crossed = b if crossed is None else crossed + b
    half = B * B
    lane = lax.broadcasted_iota(jnp.int32, crossed.shape, 1)
    crossed = pltpu.roll(crossed, half, 1)
    total = (straight + jnp.where(lane < half, -crossed, crossed)).astype(out_ref.dtype)
    for cell in range(out_ref.shape[0]):
        out_ref[cell] = total


def pole_sum_call(weights, parts, copies):
    return pl.pallas_call(
        pole_sum_kernel,
        out_shape=jax.ShapeDtypeStruct((copies, SLOTS, 2 * B * B), jnp.float32),
        in_specs=[pl.BlockSpec(memory_space=pltpu.VMEM)] * 2,
        out_specs=pl.BlockSpec(memory_space=pltpu.VMEM),
        name="pole_sum",
    )(weights, parts)


def density_kernel(index_ref, sums_ref, projector_ref, out_ref):
    @pl.loop(0, out_ref.shape[0] // 16)
    def _(group):
        first = pl.multiple_of(group * 16, 16)
        for s in range(16):
            q = first + s
            out_ref[pl.ds(q, 1), :] = sums_ref[pl.ds(index_ref[q], 1), :]
        here = pl.ds(first, 16)
        out_ref[here, :] = out_ref[here, :] * projector_ref[here, :]


def density_call(index, sums, projector):
    return pl.pallas_call(
        density_kernel,
        out_shape=jax.ShapeDtypeStruct(projector.shape, jnp.float32),
        in_specs=[pl.BlockSpec(memory_space=pltpu.SMEM)]
        + [pl.BlockSpec(memory_space=pltpu.VMEM)] * 2,
        out_specs=pl.BlockSpec(memory_space=pltpu.VMEM),
        name="density",
    )(index, sums, projector)


def pair_tables(pair_row, pair_col, row, col, pole, owners):
    row_atoms, col_atoms, trail_atoms = KA // ROWS, KA // COLS, 128 // COLS
    a = pair_row.reshape(owners, -1)
    b = pair_col.reshape(owners, -1)
    in_super = a < KA
    trail = a - KA
    cell = jnp.where(
        in_super,
        (a // row_atoms) * COLS + b // col_atoms,
        (b // row_atoms) * COLS + trail // trail_atoms,
    )
    table_atom = jnp.where(in_super, a % row_atoms, row_atoms + trail % trail_atoms)
    column_atom = jnp.where(in_super, b % col_atoms, b % row_atoms)
    tile, place = column_atom // 16, column_atom % 16
    code = (tile * (row_atoms + trail_atoms) + table_atom) * 16 + place
    pairs = a.shape[1]
    place = jnp.arange(pairs, dtype=jnp.int32)
    earlier = place[:, None] < place[None, :]
    mine = cell == row * COLS + col
    rank = jnp.dot(
        mine.astype(jnp.bfloat16),
        earlier.astype(jnp.bfloat16),
        preferred_element_type=jnp.float32,
    ).astype(jnp.int32)
    slot = jnp.where(mine, rank, -1)
    hit = slot[:, None, :] == jnp.arange(SLOTS, dtype=jnp.int32)[None, :, None]
    codes = jnp.sum(jnp.where(hit, code[:, None, :], 0), axis=2).reshape(owners * SLOTS)
    own_cell = lax.dynamic_index_in_dim(cell, pole, 0, keepdims=False)
    same = (own_cell[:, None] == own_cell[None, :]) & earlier
    index = own_cell * SLOTS + jnp.sum(same.astype(jnp.int32), axis=0)
    return codes, index


def local(
    inverse_trail, lower_t, diag_inverse, pole_weight, pole_slot, pair_row, pair_col, projector
):
    row = lax.axis_index("row")
    col = lax.axis_index("col")
    pole = lax.axis_index(POLE)
    poles = lax.axis_size(POLE)
    base = ((row - col + COLS) % COLS).astype(jnp.int32).reshape(1)

    trail = parts_apart(inverse_trail[0])
    lower = parts_apart(lower_t[0])
    lower, trail = lax.optimization_barrier((lower, trail))

    trails = [trail] + [lax.ppermute(trail, "row", ring(e, ROWS)) for e in range(1, ROWS)]
    lefts = [lax.ppermute(lower, ("row", "col"), to_process_rows(d)) for d in range(COLS)]

    codes, index = pair_tables(pair_row, pair_col, row, col, pole, poles)
    diag = parts_apart(diag_inverse[0])
    wide_projector = jnp.concatenate([projector, projector], axis=1).astype(jnp.float32)
    masks = (
        jnp.arange(16, dtype=jnp.int32)[:, None, None]
        == jnp.broadcast_to(jnp.arange(128, dtype=jnp.int32) // B, (16, 128))[None]
    ).astype(jnp.bfloat16)

    coupling, coupling_t = coupling_call(base, lefts, trails)
    lower_late, coupling = lax.optimization_barrier((lower, coupling))
    couplings = [coupling] + [
        lax.ppermute(coupling, "col", ring(d, COLS)) for d in range(1, COLS)
    ]
    lowers = [lower] + [lax.ppermute(lower_late, "row", ring(e, ROWS)) for e in range(1, ROWS)]

    block, pairs = block_call(
        base, pole_slot, codes, couplings, lowers, diag, coupling_t, masks
    )
    out = block.transpose(1, 0, 2)[None]

    parts = lax.all_to_all(pairs, POLE, 0, 0, tiled=True)
    cells = ROWS * COLS
    summed = pole_sum_call(pole_weight.T, parts, cells)
    everywhere = lax.all_to_all(summed, ("row", "col"), 0, 0, tiled=True)
    density = density_call(index, everywhere.reshape(cells * SLOTS, 2 * B * B), wide_projector)
    return (out, density)


def solution(mesh):
    split = Mesh(
        mesh.devices.reshape(8, 2, mesh.shape["row"], mesh.shape["col"]),
        ("pole_0", "pole_1", "row", "col"),
    )
    in_specs = (
        P(POLE, "row", None, "col"),
        P(POLE, "col", None, "row"),
        P(POLE, "row", None, "col"),
        P(),
        P(POLE),
        P(),
        P(),
        P(POLE, None),
    )
    out_specs = (P(POLE, "row", None, "col"), P(POLE, None))
    return jax.shard_map(local, mesh=split, in_specs=in_specs, out_specs=out_specs, check_vma=False)
```

```python
import jax
import jax.numpy as jnp
from jax import lax
from jax.experimental import pallas as pl
from jax.experimental.pallas import tpu as pltpu
from jax.sharding import Mesh
from jax.sharding import PartitionSpec as P

B = 8
KA = 256
POLE = ("pole_0", "pole_1")
ROWS = 4
COLS = 4
SLOTS = 64
GROUP = 32
MIB = 1 << 20


def ring(shift, peers):
    return [(i, (i + shift) % peers) for i in range(peers)]


def to_process_rows(shift):
    return [
        (k * COLS + x, x * COLS + (k + shift) % COLS) for k in range(ROWS) for x in range(COLS)
    ]


def parts_apart(raw):
    return raw.transpose(1, 0, 2)


def whole(shape):
    return pl.BlockSpec(shape, lambda *_: (0,) * len(shape))


def product(left, right, dim):
    return lax.dot_general(
        left, right, (((1,), (dim,)), ((), ())), preferred_element_type=jnp.float32
    )


def complex_product(lefts, rights, dim, order):
    left = jnp.concatenate([x[...].reshape(-1, x.shape[2]) for x in lefts], axis=1)
    real = jnp.concatenate([rights[e][0] for e in order], axis=dim)
    imag = jnp.concatenate([rights[e][1] for e in order], axis=dim)
    half = left.shape[0] // 2
    u = product(left, real, dim)
    v = product(left, imag, dim)
    return u[:half] - v[half:], u[half:] + v[:half]


def by_atom(re, im):
    rows, columns = re.shape
    pair = [x.reshape(rows // B, B, columns) for x in (re, im)]
    return jnp.stack(pair, axis=1).reshape(2 * rows, columns).astype(jnp.bfloat16)


def coupling_kernel(base_ref, l0, l1, l2, l3, t0, t1, t2, t3, c_ref, ct_ref):
    def run(order):
        re, im = complex_product((l0, l1, l2, l3), (t0, t1, t2, t3), 0, order)
        c_ref[0] = (-re).astype(jnp.bfloat16)
        c_ref[1] = (-im).astype(jnp.bfloat16)
        ct_ref[...] = by_atom((-re).T, (-im).T)

    for base in range(ROWS):

        @pl.when(base_ref[0] == base)
        def _():
            run([(base + d) % ROWS for d in range(ROWS)])


def coupling_call(base, lefts, trails):
    _, rows, inner = lefts[0].shape
    columns = trails[0].shape[2]
    tile = 256
    left_spec = pl.BlockSpec((2, tile, inner), lambda i, *_: (0, i, 0))
    return pl.pallas_call(
        coupling_kernel,
        out_shape=(
            jax.ShapeDtypeStruct((2, rows, columns), jnp.bfloat16),
            jax.ShapeDtypeStruct((2 * columns, rows), jnp.bfloat16),
        ),
        grid_spec=pltpu.PrefetchScalarGridSpec(
            num_scalar_prefetch=1,
            grid=(rows // tile,),
            in_specs=[left_spec] * 4 + [whole(trails[0].shape)] * 4,
            out_specs=(
                pl.BlockSpec((2, tile, columns), lambda i, *_: (0, i, 0)),
                pl.BlockSpec((2 * columns, tile), lambda i, *_: (0, i)),
            ),
        ),
        compiler_params=pltpu.CompilerParams(vmem_limit_bytes=14 * MIB),
        cost_estimate=pl.CostEstimate(
            flops=2 * rows * inner * 16 * columns, bytes_accessed=6 << 20, transcendentals=0
        ),
        name="coupling",
    )(base, *lefts, *trails)


def take_pairs(codes_ref, mask_ref, pairs_ref, table, lanes, spread, keep, fold):
    owners = pairs_ref.shape[0]

    @pl.loop(0, owners * SLOTS // GROUP)
    def _(group):
        first = group * GROUP
        to = pl.multiple_of(first * 16, GROUP * 16)
        for s in range(GROUP):
            code = codes_ref[first + s]
            found = table[pl.ds(pl.multiple_of(code & ~15, 16), 16), :]
            lanes[pl.ds(to + s * 16, 16), :] = found * mask_ref[code & 15]

    many = 4

    @pl.loop(0, owners // many)
    def _(chunk):
        rows = many * SLOTS * 16
        wide = product(lanes[pl.ds(pl.multiple_of(chunk * rows, rows), rows), :], spread[...], 0)
        wide = wide.reshape(many * SLOTS, 2, 8, 2 * B * B) * keep[...][None]
        wide = (wide[:, 0] + wide[:, 1]).reshape(many, SLOTS * 8, 2 * B * B).astype(jnp.bfloat16)
        for o in range(many):
            pairs_ref[chunk * many + o, :SLOTS, :] = product(fold[...], wide[o], 0).astype(
                jnp.bfloat16
            )


def block_kernel(
    base_ref, slot_ref, codes_ref, c0, c1, c2, c3, l0, l1, l2, l3, diag_ref, ct_ref, mask_ref,
    out_ref, pairs_ref, table, lanes, spread, keep, fold,
):
    step = pl.program_id(0)
    last = pl.num_programs(0) - 1
    tile = out_ref.shape[1]
    per_tile = table.shape[0] // 4
    super_rows = per_tile - ct_ref.shape[0]

    @pl.when(step == 0)
    def _():
        for t in range(4):
            first = t * per_tile + super_rows
            table[first : first + ct_ref.shape[0], :] = ct_ref[:, t * 128 : t * 128 + 128]
        lane = lax.broadcasted_iota(jnp.int32, (128, 128), 1)
        row = lax.broadcasted_iota(jnp.int32, (128, 128), 0)
        spread[...] = jnp.where(row % 8 == lane % 8, 1.0, 0.0).astype(jnp.bfloat16)
        part = lax.broadcasted_iota(jnp.int32, (2, 8, 128), 0)
        row = lax.broadcasted_iota(jnp.int32, (2, 8, 128), 1)
        lane = lax.broadcasted_iota(jnp.int32, (2, 8, 128), 2)
        keep[...] = jnp.where(lane // 8 == part * 8 + row, 1.0, 0.0)
        row = lax.broadcasted_iota(jnp.int32, fold.shape, 0)
        lane = lax.broadcasted_iota(jnp.int32, fold.shape, 1)
        fold[...] = jnp.where(lane // 8 == row, 1.0, 0.0).astype(jnp.bfloat16)
        slot = jnp.full((16, 128), slot_ref[0], jnp.int32).astype(jnp.float32)
        for owner in range(pairs_ref.shape[0]):
            pairs_ref[owner, SLOTS:, :] = slot.astype(jnp.bfloat16)

    def run(order):
        re, im = complex_product((c0, c1, c2, c3), (l0, l1, l2, l3), 1, order)
        re = diag_ref[0].astype(jnp.float32) - re
        im = diag_ref[1].astype(jnp.float32) - im
        out_ref[0] = re.astype(jnp.bfloat16)
        out_ref[1] = im.astype(jnp.bfloat16)
        rows = by_atom(re, im)
        for t in range(4):
            first = pl.multiple_of(t * per_tile + step * 2 * tile, 2 * tile)
            table[pl.ds(first, 2 * tile), :] = rows[:, t * 128 : t * 128 + 128]

    for base in range(ROWS):

        @pl.when(base_ref[0] == base)
        def _():
            run([(base + d) % ROWS for d in range(ROWS)])

    @pl.when(step == last)
    def _():
        take_pairs(codes_ref, mask_ref, pairs_ref, table, lanes, spread, keep, fold)


def block_call(base, slot, codes, couplings, lowers, diag, coupling_t, masks):
    _, rows, columns = diag.shape
    inner = couplings[0].shape[2]
    owners = codes.shape[0] // SLOTS
    tile = 256
    row_spec = lambda last: pl.BlockSpec((2, tile, last), lambda i, *_: (0, i, 0))
    return pl.pallas_call(
        block_kernel,
        out_shape=(
            jax.ShapeDtypeStruct((2, rows, columns), jnp.bfloat16),
            jax.ShapeDtypeStruct((owners, SLOTS + 16, 2 * B * B), jnp.bfloat16),
        ),
        grid_spec=pltpu.PrefetchScalarGridSpec(
            num_scalar_prefetch=3,
            grid=(rows // tile,),
            in_specs=[row_spec(inner)] * 4
            + [whole(lowers[0].shape)] * 4
            + [row_spec(columns), whole(coupling_t.shape), whole(masks.shape)],
            out_specs=(row_spec(columns), whole((owners, SLOTS + 16, 2 * B * B))),
            scratch_shapes=[
                pltpu.VMEM((4 * (2 * rows + coupling_t.shape[0]), 128), jnp.bfloat16),
                pltpu.VMEM((owners * SLOTS * 16, 128), jnp.bfloat16),
                pltpu.VMEM((128, 128), jnp.bfloat16),
                pltpu.VMEM((2, 8, 128), jnp.float32),
                pltpu.VMEM((SLOTS, SLOTS * 8), jnp.bfloat16),
            ],
        ),
        compiler_params=pltpu.CompilerParams(vmem_limit_bytes=24 * MIB),
        cost_estimate=pl.CostEstimate(
            flops=2 * rows * inner * 16 * columns, bytes_accessed=12 << 20, transcendentals=0
        ),
        name="block_and_pairs",
    )(base, slot, codes, *couplings, *lowers, diag, coupling_t, masks)


def pole_sum_kernel(weight_ref, parts_ref, out_ref):
    lane = lax.broadcasted_iota(jnp.int32, (1, 128), 1).astype(jnp.float32)
    straight = crossed = None
    for p in range(parts_ref.shape[0]):
        part = parts_ref[p, :SLOTS, :].astype(jnp.float32)
        slot = parts_ref[p, SLOTS:, :].astype(jnp.float32)[:1]
        weight = []
        for c in range(2):
            found = jnp.where(slot == lane, weight_ref[c : c + 1, :128], 0.0) + jnp.where(
                slot == lane + 128.0, weight_ref[c : c + 1, 128:], 0.0
            )
            weight.append(jnp.sum(found, axis=1, keepdims=True))
        a = weight[0] * part
        b = weight[1] * part
        straight = a if straight is None else straight + a
        crossed = b if crossed is None else crossed + b
    half = B * B
    lane = lax.broadcasted_iota(jnp.int32, crossed.shape, 1)
    crossed = pltpu.roll(crossed, half, 1)
    total = (straight + jnp.where(lane < half, -crossed, crossed)).astype(out_ref.dtype)
    for cell in range(out_ref.shape[0]):
        out_ref[cell] = total


def pole_sum_call(weights, parts, copies):
    return pl.pallas_call(
        pole_sum_kernel,
        out_shape=jax.ShapeDtypeStruct((copies, SLOTS, 2 * B * B), jnp.bfloat16),
        in_specs=[pl.BlockSpec(memory_space=pltpu.VMEM)] * 2,
        out_specs=pl.BlockSpec(memory_space=pltpu.VMEM),
        compiler_params=pltpu.CompilerParams(vmem_limit_bytes=6 * MIB),
        name="pole_sum",
    )(weights, parts)


def density_kernel(index_ref, sums_ref, projector_ref, out_ref, sums):
    sums[...] = sums_ref[...].astype(jnp.float32)

    @pl.loop(0, out_ref.shape[0] // 32)
    def _(group):
        first = pl.multiple_of(group * 32, 32)
        for s in range(32):
            q = first + s
            out_ref[pl.ds(q, 1), :] = sums[pl.ds(index_ref[q], 1), :]

    out_ref[...] = out_ref[...] * projector_ref[...]


def density_call(index, sums, projector):
    return pl.pallas_call(
        density_kernel,
        out_shape=jax.ShapeDtypeStruct(projector.shape, jnp.float32),
        in_specs=[pl.BlockSpec(memory_space=pltpu.SMEM)]
        + [pl.BlockSpec(memory_space=pltpu.VMEM)] * 2,
        out_specs=pl.BlockSpec(memory_space=pltpu.VMEM),
        scratch_shapes=[pltpu.VMEM(sums.shape, jnp.float32)],
        compiler_params=pltpu.CompilerParams(vmem_limit_bytes=6 * MIB),
        name="density",
    )(index, sums, projector)


def pair_tables(pair_row, pair_col, row, col, pole, owners):
    row_atoms, col_atoms, trail_atoms = KA // ROWS, KA // COLS, 128 // COLS
    a = pair_row.reshape(owners, -1)
    b = pair_col.reshape(owners, -1)
    in_super = a < KA
    trail = a - KA
    cell = jnp.where(
        in_super,
        (a // row_atoms) * COLS + b // col_atoms,
        (b // row_atoms) * COLS + trail // trail_atoms,
    )
    table_atom = jnp.where(in_super, a % row_atoms, row_atoms + trail % trail_atoms)
    column_atom = jnp.where(in_super, b % col_atoms, b % row_atoms)
    tile, place = column_atom // 16, column_atom % 16
    code = (tile * (row_atoms + trail_atoms) + table_atom) * 16 + place
    pairs = a.shape[1]
    place = jnp.arange(pairs, dtype=jnp.int32)
    earlier = place[:, None] < place[None, :]
    mine = cell == row * COLS + col
    rank = jnp.dot(
        mine.astype(jnp.bfloat16),
        earlier.astype(jnp.bfloat16),
        preferred_element_type=jnp.float32,
    ).astype(jnp.int32)
    slot = jnp.where(mine, rank, -1)
    hit = slot[:, None, :] == jnp.arange(SLOTS, dtype=jnp.int32)[None, :, None]
    codes = jnp.sum(jnp.where(hit, code[:, None, :], 0), axis=2).reshape(owners * SLOTS)
    own_cell = lax.dynamic_index_in_dim(cell, pole, 0, keepdims=False)
    same = (own_cell[:, None] == own_cell[None, :]) & earlier
    index = own_cell * SLOTS + jnp.sum(same.astype(jnp.int32), axis=0)
    return codes, index


def local(
    inverse_trail, lower_t, diag_inverse, pole_weight, pole_slot, pair_row, pair_col, projector
):
    row = lax.axis_index("row")
    col = lax.axis_index("col")
    pole = lax.axis_index(POLE)
    poles = lax.axis_size(POLE)
    base = ((row - col + COLS) % COLS).astype(jnp.int32).reshape(1)

    trail = parts_apart(inverse_trail[0])
    lower = parts_apart(lower_t[0])
    lower, trail = lax.optimization_barrier((lower, trail))

    trails = [trail] + [lax.ppermute(trail, "row", ring(e, ROWS)) for e in range(1, ROWS)]
    lefts = [lax.ppermute(lower, ("row", "col"), to_process_rows(d)) for d in range(COLS)]

    codes, index = pair_tables(pair_row, pair_col, row, col, pole, poles)
    diag = parts_apart(diag_inverse[0])
    wide_projector = jnp.concatenate([projector, projector], axis=1).astype(jnp.float32)
    masks = (
        jnp.arange(16, dtype=jnp.int32)[:, None, None]
        == jnp.broadcast_to(jnp.arange(128, dtype=jnp.int32) // B, (16, 128))[None]
    ).astype(jnp.bfloat16)

    coupling, coupling_t = coupling_call(base, lefts, trails)
    lower_late, coupling = lax.optimization_barrier((lower, coupling))
    couplings = [coupling] + [
        lax.ppermute(coupling, "col", ring(d, COLS)) for d in range(1, COLS)
    ]
    lowers = [lower] + [lax.ppermute(lower_late, "row", ring(e, ROWS)) for e in range(1, ROWS)]

    block, pairs = block_call(
        base, pole_slot, codes, couplings, lowers, diag, coupling_t, masks
    )
    out = block.transpose(1, 0, 2)[None]

    parts = lax.all_to_all(pairs, POLE, 0, 0, tiled=True)
    cells = ROWS * COLS
    summed = pole_sum_call(pole_weight.T, parts, cells)
    everywhere = lax.all_to_all(summed, ("row", "col"), 0, 0, tiled=True)
    density = density_call(index, everywhere.reshape(cells * SLOTS, 2 * B * B), wide_projector)
    return (out, density)


def solution(mesh):
    split = Mesh(
        mesh.devices.reshape(8, 2, mesh.shape["row"], mesh.shape["col"]),
        ("pole_0", "pole_1", "row", "col"),
    )
    in_specs = (
        P(POLE, "row", None, "col"),
        P(POLE, "col", None, "row"),
        P(POLE, "row", None, "col"),
        P(),
        P(POLE),
        P(),
        P(),
        P(POLE, None),
    )
    out_specs = (P(POLE, "row", None, "col"), P(POLE, None))
    return jax.shard_map(local, mesh=split, in_specs=in_specs, out_specs=out_specs, check_vma=False)
```

```python
import jax
import jax.numpy as jnp
from jax import lax
from jax.experimental import pallas as pl
from jax.experimental.pallas import tpu as pltpu
from jax.sharding import Mesh
from jax.sharding import PartitionSpec as P

B = 8
KA = 256
POLE = ("pole_0", "pole_1")
ROWS = 4
COLS = 4
SLOTS = 64
GROUP = 32
MIB = 1 << 20


def ring(shift, peers):
    return [(i, (i + shift) % peers) for i in range(peers)]


def along_row(e):
    return [
        (k * COLS + x, k * COLS + (x - k - e) % COLS) for k in range(ROWS) for x in range(COLS)
    ]


def along_column(e):
    return [
        (k * COLS + c, (c + k + e) % ROWS * COLS + c) for k in range(ROWS) for c in range(COLS)
    ]


def parts_apart(raw):
    return raw.transpose(1, 0, 2)


def whole(shape):
    return pl.BlockSpec(shape, lambda *_: (0,) * len(shape))


def product(left, right, dim):
    return lax.dot_general(
        left, right, (((1,), (dim,)), ((), ())), preferred_element_type=jnp.float32
    )


def complex_product(lefts, rights, dim, order):
    left = jnp.concatenate([x[...].reshape(-1, x.shape[2]) for x in lefts], axis=1)
    real = jnp.concatenate([rights(e)[0] for e in order], axis=dim)
    imag = jnp.concatenate([rights(e)[1] for e in order], axis=dim)
    half = left.shape[0] // 2
    u = product(left, real, dim)
    v = product(left, imag, dim)
    return u[:half] - v[half:], u[half:] + v[:half]


def by_atom(re, im):
    rows, columns = re.shape
    pair = [x.reshape(rows // B, B, columns) for x in (re, im)]
    return jnp.stack(pair, axis=1).reshape(2 * rows, columns).astype(jnp.bfloat16)


def coupling_kernel(base_ref, l0, l1, l2, l3, t_ref, c_ref, ct_ref):
    def run(order):
        re, im = complex_product((l0, l1, l2, l3), t_ref.at.__getitem__, 0, order)
        c_ref[0] = (-re).astype(jnp.bfloat16)
        c_ref[1] = (-im).astype(jnp.bfloat16)
        ct_ref[...] = by_atom((-re).T, (-im).T)

    for base in range(ROWS):

        @pl.when(base_ref[0] == base)
        def _():
            run([(base - e) % ROWS for e in range(ROWS)])


def coupling_call(base, lefts, trail):
    _, rows, inner = lefts[0].shape
    columns = trail.shape[3]
    tile = 256
    left_spec = pl.BlockSpec((2, tile, inner), lambda i, *_: (0, i, 0))
    return pl.pallas_call(
        coupling_kernel,
        out_shape=(
            jax.ShapeDtypeStruct((2, rows, columns), jnp.bfloat16),
            jax.ShapeDtypeStruct((2 * columns, rows), jnp.bfloat16),
        ),
        grid_spec=pltpu.PrefetchScalarGridSpec(
            num_scalar_prefetch=1,
            grid=(rows // tile,),
            in_specs=[left_spec] * 4 + [whole(trail.shape)],
            out_specs=(
                pl.BlockSpec((2, tile, columns), lambda i, *_: (0, i, 0)),
                pl.BlockSpec((2 * columns, tile), lambda i, *_: (0, i)),
            ),
        ),
        compiler_params=pltpu.CompilerParams(vmem_limit_bytes=14 * MIB),
        cost_estimate=pl.CostEstimate(
            flops=2 * rows * inner * 16 * columns, bytes_accessed=6 << 20, transcendentals=0
        ),
        name="coupling",
    )(base, *lefts, trail)


def take_pairs(codes_ref, mask_ref, pairs_ref, table, lanes, spread, keep, fold):
    owners = pairs_ref.shape[0]

    @pl.loop(0, owners * SLOTS // GROUP)
    def _(group):
        first = group * GROUP
        to = pl.multiple_of(first * 16, GROUP * 16)
        for s in range(GROUP):
            code = codes_ref[first + s]
            found = table[pl.ds(pl.multiple_of(code & ~15, 16), 16), :]
            lanes[pl.ds(to + s * 16, 16), :] = found * mask_ref[code & 15]

    many = 4

    @pl.loop(0, owners // many)
    def _(chunk):
        rows = many * SLOTS * 16
        wide = product(lanes[pl.ds(pl.multiple_of(chunk * rows, rows), rows), :], spread[...], 0)
        wide = wide.reshape(many * SLOTS, 2, 8, 2 * B * B) * keep[...][None]
        wide = (wide[:, 0] + wide[:, 1]).reshape(many, SLOTS * 8, 2 * B * B).astype(jnp.bfloat16)
        for o in range(many):
            pairs_ref[chunk * many + o, :SLOTS, :] = product(fold[...], wide[o], 0).astype(
                jnp.bfloat16
            )


def block_kernel(
    base_ref, slot_ref, codes_ref, c0, c1, c2, c3, l0, l1, l2, l3, diag_ref, ct_ref, mask_ref,
    out_ref, pairs_ref, table, lanes, spread, keep, fold,
):
    step = pl.program_id(0)
    last = pl.num_programs(0) - 1
    tile = out_ref.shape[1]
    per_tile = table.shape[0] // 4
    super_rows = per_tile - ct_ref.shape[0]

    @pl.when(step == 0)
    def _():
        for t in range(4):
            first = t * per_tile + super_rows
            table[first : first + ct_ref.shape[0], :] = ct_ref[:, t * 128 : t * 128 + 128]
        lane = lax.broadcasted_iota(jnp.int32, (128, 128), 1)
        row = lax.broadcasted_iota(jnp.int32, (128, 128), 0)
        spread[...] = jnp.where(row % 8 == lane % 8, 1.0, 0.0).astype(jnp.bfloat16)
        part = lax.broadcasted_iota(jnp.int32, (2, 8, 128), 0)
        row = lax.broadcasted_iota(jnp.int32, (2, 8, 128), 1)
        lane = lax.broadcasted_iota(jnp.int32, (2, 8, 128), 2)
        keep[...] = jnp.where(lane // 8 == part * 8 + row, 1.0, 0.0)
        row = lax.broadcasted_iota(jnp.int32, fold.shape, 0)
        lane = lax.broadcasted_iota(jnp.int32, fold.shape, 1)
        fold[...] = jnp.where(lane // 8 == row, 1.0, 0.0).astype(jnp.bfloat16)
        slot = jnp.full((16, 128), slot_ref[0], jnp.int32).astype(jnp.float32)
        for owner in range(pairs_ref.shape[0]):
            pairs_ref[owner, SLOTS:, :] = slot.astype(jnp.bfloat16)

    def run(order):
        re, im = complex_product((c0, c1, c2, c3), (l0, l1, l2, l3).__getitem__, 1, order)
        re = diag_ref[0].astype(jnp.float32) - re
        im = diag_ref[1].astype(jnp.float32) - im
        out_ref[0] = re.astype(jnp.bfloat16)
        out_ref[1] = im.astype(jnp.bfloat16)
        rows = by_atom(re, im)
        for t in range(4):
            first = pl.multiple_of(t * per_tile + step * 2 * tile, 2 * tile)
            table[pl.ds(first, 2 * tile), :] = rows[:, t * 128 : t * 128 + 128]

    for base in range(ROWS):

        @pl.when(base_ref[0] == base)
        def _():
            run([(base + d) % ROWS for d in range(ROWS)])

    @pl.when(step == last)
    def _():
        take_pairs(codes_ref, mask_ref, pairs_ref, table, lanes, spread, keep, fold)


def block_call(base, slot, codes, couplings, lowers, diag, coupling_t, masks):
    _, rows, columns = diag.shape
    inner = couplings[0].shape[2]
    owners = codes.shape[0] // SLOTS
    tile = 256
    row_spec = lambda last: pl.BlockSpec((2, tile, last), lambda i, *_: (0, i, 0))
    return pl.pallas_call(
        block_kernel,
        out_shape=(
            jax.ShapeDtypeStruct((2, rows, columns), jnp.bfloat16),
            jax.ShapeDtypeStruct((owners, SLOTS + 16, 2 * B * B), jnp.bfloat16),
        ),
        grid_spec=pltpu.PrefetchScalarGridSpec(
            num_scalar_prefetch=3,
            grid=(rows // tile,),
            in_specs=[row_spec(inner)] * 4
            + [whole(lowers[0].shape)] * 4
            + [row_spec(columns), whole(coupling_t.shape), whole(masks.shape)],
            out_specs=(row_spec(columns), whole((owners, SLOTS + 16, 2 * B * B))),
            scratch_shapes=[
                pltpu.VMEM((4 * (2 * rows + coupling_t.shape[0]), 128), jnp.bfloat16),
                pltpu.VMEM((owners * SLOTS * 16, 128), jnp.bfloat16),
                pltpu.VMEM((128, 128), jnp.bfloat16),
                pltpu.VMEM((2, 8, 128), jnp.float32),
                pltpu.VMEM((SLOTS, SLOTS * 8), jnp.bfloat16),
            ],
        ),
        compiler_params=pltpu.CompilerParams(vmem_limit_bytes=60 * MIB),
        cost_estimate=pl.CostEstimate(
            flops=2 * rows * inner * 16 * columns, bytes_accessed=12 << 20, transcendentals=0
        ),
        name="block_and_pairs",
    )(base, slot, codes, *couplings, *lowers, diag, coupling_t, masks)


def pole_sum_kernel(weight_ref, parts_ref, out_ref):
    lane = lax.broadcasted_iota(jnp.int32, (1, 128), 1).astype(jnp.float32)
    straight = crossed = None
    for p in range(parts_ref.shape[0]):
        part = parts_ref[p, :SLOTS, :].astype(jnp.float32)
        slot = parts_ref[p, SLOTS:, :].astype(jnp.float32)[:1]
        weight = []
        for c in range(2):
            found = jnp.where(slot == lane, weight_ref[c : c + 1, :128], 0.0) + jnp.where(
                slot == lane + 128.0, weight_ref[c : c + 1, 128:], 0.0
            )
            weight.append(jnp.sum(found, axis=1, keepdims=True))
        a = weight[0] * part
        b = weight[1] * part
        straight = a if straight is None else straight + a
        crossed = b if crossed is None else crossed + b
    half = B * B
    lane = lax.broadcasted_iota(jnp.int32, crossed.shape, 1)
    crossed = pltpu.roll(crossed, half, 1)
    total = (straight + jnp.where(lane < half, -crossed, crossed)).astype(out_ref.dtype)
    for cell in range(out_ref.shape[0]):
        out_ref[cell] = total


def pole_sum_call(weights, parts, copies):
    return pl.pallas_call(
        pole_sum_kernel,
        out_shape=jax.ShapeDtypeStruct((copies, SLOTS, 2 * B * B), jnp.bfloat16),
        in_specs=[pl.BlockSpec(memory_space=pltpu.VMEM)] * 2,
        out_specs=pl.BlockSpec(memory_space=pltpu.VMEM),
        compiler_params=pltpu.CompilerParams(vmem_limit_bytes=6 * MIB),
        name="pole_sum",
    )(weights, parts)


def density_kernel(index_ref, sums_ref, projector_ref, out_ref, sums):
    sums[...] = sums_ref[...].astype(jnp.float32)

    @pl.loop(0, out_ref.shape[0] // 32)
    def _(group):
        first = pl.multiple_of(group * 32, 32)
        for s in range(32):
            q = first + s
            out_ref[pl.ds(q, 1), :] = sums[pl.ds(index_ref[q], 1), :]

    out_ref[...] = out_ref[...] * projector_ref[...]


def density_call(index, sums, projector):
    return pl.pallas_call(
        density_kernel,
        out_shape=jax.ShapeDtypeStruct(projector.shape, jnp.float32),
        in_specs=[pl.BlockSpec(memory_space=pltpu.SMEM)]
        + [pl.BlockSpec(memory_space=pltpu.VMEM)] * 2,
        out_specs=pl.BlockSpec(memory_space=pltpu.VMEM),
        scratch_shapes=[pltpu.VMEM(sums.shape, jnp.float32)],
        compiler_params=pltpu.CompilerParams(vmem_limit_bytes=6 * MIB),
        name="density",
    )(index, sums, projector)


def pair_tables(pair_row, pair_col, row, col, pole, owners):
    row_atoms, col_atoms, trail_atoms = KA // ROWS, KA // COLS, 128 // COLS
    a = pair_row.reshape(owners, -1)
    b = pair_col.reshape(owners, -1)
    in_super = a < KA
    trail = a - KA
    cell = jnp.where(
        in_super,
        (a // row_atoms) * COLS + b // col_atoms,
        (b // row_atoms) * COLS + trail // trail_atoms,
    )
    table_atom = jnp.where(in_super, a % row_atoms, row_atoms + trail % trail_atoms)
    column_atom = jnp.where(in_super, b % col_atoms, b % row_atoms)
    tile, place = column_atom // 16, column_atom % 16
    code = (tile * (row_atoms + trail_atoms) + table_atom) * 16 + place
    pairs = a.shape[1]
    place = jnp.arange(pairs, dtype=jnp.int32)
    earlier = place[:, None] < place[None, :]
    mine = cell == row * COLS + col
    rank = jnp.dot(
        mine.astype(jnp.bfloat16),
        earlier.astype(jnp.bfloat16),
        preferred_element_type=jnp.float32,
    ).astype(jnp.int32)
    slot = jnp.where(mine, rank, -1)
    hit = slot[:, None, :] == jnp.arange(SLOTS, dtype=jnp.int32)[None, :, None]
    codes = jnp.sum(jnp.where(hit, code[:, None, :], 0), axis=2).reshape(owners * SLOTS)
    own_cell = lax.dynamic_index_in_dim(cell, pole, 0, keepdims=False)
    same = (own_cell[:, None] == own_cell[None, :]) & earlier
    index = own_cell * SLOTS + jnp.sum(same.astype(jnp.int32), axis=0)
    return codes, index


def local(
    inverse_trail, lower_t, diag_inverse, pole_weight, pole_slot, pair_row, pair_col, projector
):
    row = lax.axis_index("row")
    col = lax.axis_index("col")
    pole = lax.axis_index(POLE)
    poles = lax.axis_size(POLE)
    base = ((row - col + COLS) % COLS).astype(jnp.int32).reshape(1)

    trail = parts_apart(inverse_trail[0])
    lower = parts_apart(lower_t[0])
    lower, trail = lax.optimization_barrier((lower, trail))

    pair_axes = ("row", "col")
    trail_all = lax.all_gather(trail[None], "row", axis=0, tiled=True)
    lefts = [lax.ppermute(lower, pair_axes, along_row(e)) for e in range(COLS)]
    lower_first = lax.ppermute(lower, "row", ring(1, ROWS))
    lefts = [lax.ppermute(left, pair_axes, along_column(e)) for e, left in enumerate(lefts)]

    codes, index = pair_tables(pair_row, pair_col, row, col, pole, poles)
    diag = parts_apart(diag_inverse[0])
    wide_projector = jnp.concatenate([projector, projector], axis=1).astype(jnp.float32)
    masks = (
        jnp.arange(16, dtype=jnp.int32)[:, None, None]
        == jnp.broadcast_to(jnp.arange(128, dtype=jnp.int32) // B, (16, 128))[None]
    ).astype(jnp.bfloat16)

    coupling, coupling_t = coupling_call(base, lefts, trail_all)
    lower_late, coupling = lax.optimization_barrier((lower, coupling))
    couplings = [coupling] + [
        lax.ppermute(coupling, "col", ring(d, COLS)) for d in range(1, COLS)
    ]
    lowers = [lower, lower_first] + [
        lax.ppermute(lower_late, "row", ring(e, ROWS)) for e in range(2, ROWS)
    ]

    block, pairs = block_call(
        base, pole_slot, codes, couplings, lowers, diag, coupling_t, masks
    )
    out = block.transpose(1, 0, 2)[None]

    parts = lax.all_to_all(pairs, POLE, 0, 0, tiled=True)
    cells = ROWS * COLS
    summed = pole_sum_call(pole_weight.T, parts, cells)
    everywhere = lax.all_to_all(summed, ("row", "col"), 0, 0, tiled=True)
    density = density_call(index, everywhere.reshape(cells * SLOTS, 2 * B * B), wide_projector)
    return (out, density)


def solution(mesh):
    split = Mesh(
        mesh.devices.reshape(8, 2, mesh.shape["row"], mesh.shape["col"]),
        ("pole_0", "pole_1", "row", "col"),
    )
    in_specs = (
        P(POLE, "row", None, "col"),
        P(POLE, "col", None, "row"),
        P(POLE, "row", None, "col"),
        P(),
        P(POLE),
        P(),
        P(),
        P(POLE, None),
    )
    out_specs = (P(POLE, "row", None, "col"), P(POLE, None))
    return jax.shard_map(local, mesh=split, in_specs=in_specs, out_specs=out_specs, check_vma=False)
```

```python
import jax
import jax.numpy as jnp
from jax import lax
from jax.experimental import pallas as pl
from jax.experimental.pallas import tpu as pltpu
from jax.sharding import Mesh
from jax.sharding import PartitionSpec as P

B = 8
KA = 256
POLE = ("pole_0", "pole_1")
ROWS = 4
COLS = 4
SLOTS = 64
GROUP = 16
MIB = 1 << 20


def ring(shift, peers):
    return [(i, (i + shift) % peers) for i in range(peers)]


def to_process_rows(shift):
    return [
        (k * COLS + x, x * COLS + (k + shift) % COLS) for k in range(ROWS) for x in range(COLS)
    ]


def parts_apart(raw):
    return raw.transpose(1, 0, 2)


def whole(shape):
    return pl.BlockSpec(shape, lambda *_: (0,) * len(shape))


def product(left, right, dim):
    return lax.dot_general(
        left, right, (((1,), (dim,)), ((), ())), preferred_element_type=jnp.float32
    )


def complex_product(lefts, rights, dim, order):
    left = jnp.concatenate([x[...].reshape(-1, x.shape[2]) for x in lefts], axis=1)
    real = jnp.concatenate([rights[e][0] for e in order], axis=dim)
    imag = jnp.concatenate([rights[e][1] for e in order], axis=dim)
    half = left.shape[0] // 2
    u = product(left, real, dim)
    v = product(left, imag, dim)
    return u[:half] - v[half:], u[half:] + v[:half]


def by_atom(re, im):
    rows, columns = re.shape
    pair = [x.reshape(rows // B, B, columns) for x in (re, im)]
    return jnp.stack(pair, axis=1).reshape(2 * rows, columns).astype(jnp.bfloat16)


def coupling_kernel(base_ref, l0, l1, l2, l3, t0, t1, t2, t3, c_ref):
    def run(order):
        re, im = complex_product((l0, l1, l2, l3), (t0, t1, t2, t3), 0, order)
        c_ref[0] = (-re).astype(jnp.bfloat16)
        c_ref[1] = (-im).astype(jnp.bfloat16)

    for base in range(ROWS):

        @pl.when(base_ref[0] == base)
        def _():
            run([(base + d) % ROWS for d in range(ROWS)])


def coupling_call(base, lefts, trails):
    _, rows, inner = lefts[0].shape
    columns = trails[0].shape[2]
    tile = 256
    left_spec = pl.BlockSpec((2, tile, inner), lambda i, *_: (0, i, 0))
    return pl.pallas_call(
        coupling_kernel,
        out_shape=jax.ShapeDtypeStruct((2, rows, columns), jnp.bfloat16),
        grid_spec=pltpu.PrefetchScalarGridSpec(
            num_scalar_prefetch=1,
            grid=(rows // tile,),
            in_specs=[left_spec] * 4 + [whole(trails[0].shape)] * 4,
            out_specs=pl.BlockSpec((2, tile, columns), lambda i, *_: (0, i, 0)),
        ),
        compiler_params=pltpu.CompilerParams(vmem_limit_bytes=14 * MIB),
        cost_estimate=pl.CostEstimate(
            flops=2 * rows * inner * 16 * columns, bytes_accessed=6 << 20, transcendentals=0
        ),
        name="coupling",
    )(base, *lefts, *trails)


def take_pairs(codes_ref, counts_ref, mask_ref, pairs_ref, table, lanes, spread, keep, fold):
    owners = pairs_ref.shape[0]

    @pl.loop(0, owners * SLOTS // GROUP)
    def _(group):
        first = group * GROUP
        to = pl.multiple_of(first * 16, GROUP * 16)
        used = counts_ref[first // SLOTS] > first % SLOTS

        @pl.when(used)
        def _():
            for s in range(GROUP):
                code = codes_ref[first + s]
                found = table[pl.ds(pl.multiple_of(code & ~15, 16), 16), :]
                lanes[pl.ds(to + s * 16, 16), :] = found * mask_ref[code & 15]

        @pl.when(jnp.logical_not(used))
        def _():
            lanes[pl.ds(to, GROUP * 16), :] = jnp.zeros((GROUP * 16, 128), jnp.bfloat16)

    many = 4

    @pl.loop(0, owners // many)
    def _(chunk):
        rows = many * SLOTS * 16
        wide = product(lanes[pl.ds(pl.multiple_of(chunk * rows, rows), rows), :], spread[...], 0)
        wide = wide.reshape(many * SLOTS, 2, 8, 2 * B * B) * keep[...][None]
        wide = (wide[:, 0] + wide[:, 1]).reshape(many, SLOTS * 8, 2 * B * B).astype(jnp.bfloat16)
        for o in range(many):
            pairs_ref[chunk * many + o, :SLOTS, :] = product(fold[...], wide[o], 0).astype(
                jnp.bfloat16
            )


def block_kernel(
    base_ref, slot_ref, codes_ref, counts_ref, c0, c1, c2, c3, l0, l1, l2, l3, diag_ref, mask_ref,
    out_ref, pairs_ref, table, lanes, spread, keep, fold,
):
    step = pl.program_id(0)
    last = pl.num_programs(0) - 1
    tile = out_ref.shape[1]
    per_tile = table.shape[0] // 4
    trail_rows = 2 * c0.shape[2]
    super_rows = per_tile - trail_rows

    @pl.when(step == 0)
    def _():
        lane = lax.broadcasted_iota(jnp.int32, (128, 128), 1)
        row = lax.broadcasted_iota(jnp.int32, (128, 128), 0)
        spread[...] = jnp.where(row % 8 == lane % 8, 1.0, 0.0).astype(jnp.bfloat16)
        part = lax.broadcasted_iota(jnp.int32, (2, 8, 128), 0)
        row = lax.broadcasted_iota(jnp.int32, (2, 8, 128), 1)
        lane = lax.broadcasted_iota(jnp.int32, (2, 8, 128), 2)
        keep[...] = jnp.where(lane // 8 == part * 8 + row, 1.0, 0.0)
        row = lax.broadcasted_iota(jnp.int32, fold.shape, 0)
        lane = lax.broadcasted_iota(jnp.int32, fold.shape, 1)
        fold[...] = jnp.where(lane // 8 == row, 1.0, 0.0).astype(jnp.bfloat16)
        slot = jnp.full((16, 128), slot_ref[0], jnp.int32).astype(jnp.float32)
        for owner in range(pairs_ref.shape[0]):
            pairs_ref[owner, SLOTS:, :] = slot.astype(jnp.bfloat16)

    def run(order):
        re, im = complex_product((c0, c1, c2, c3), (l0, l1, l2, l3), 1, order)
        re = diag_ref[0].astype(jnp.float32) - re
        im = diag_ref[1].astype(jnp.float32) - im
        out_ref[0] = re.astype(jnp.bfloat16)
        out_ref[1] = im.astype(jnp.bfloat16)
        rows = by_atom(re, im)
        for t in range(4):
            first = pl.multiple_of(t * per_tile + step * 2 * tile, 2 * tile)
            table[pl.ds(first, 2 * tile), :] = rows[:, t * 128 : t * 128 + 128]
        own = [c0[part].astype(jnp.float32).T for part in range(2)]
        rows = by_atom(own[0], own[1])
        for t in range(tile // 128):
            first = pl.multiple_of((step * (tile // 128) + t) * per_tile + super_rows, trail_rows)
            table[pl.ds(first, trail_rows), :] = rows[:, t * 128 : t * 128 + 128]

    for base in range(ROWS):

        @pl.when(base_ref[0] == base)
        def _():
            run([(base + d) % ROWS for d in range(ROWS)])

    @pl.when(step == last)
    def _():
        take_pairs(codes_ref, counts_ref, mask_ref, pairs_ref, table, lanes, spread, keep, fold)


def block_call(base, slot, codes, counts, couplings, lowers, diag, masks):
    _, rows, columns = diag.shape
    inner = couplings[0].shape[2]
    owners = codes.shape[0] // SLOTS
    tile = 256
    row_spec = lambda last: pl.BlockSpec((2, tile, last), lambda i, *_: (0, i, 0))
    return pl.pallas_call(
        block_kernel,
        out_shape=(
            jax.ShapeDtypeStruct((2, rows, columns), jnp.bfloat16),
            jax.ShapeDtypeStruct((owners, SLOTS + 16, 2 * B * B), jnp.bfloat16),
        ),
        grid_spec=pltpu.PrefetchScalarGridSpec(
            num_scalar_prefetch=4,
            grid=(rows // tile,),
            in_specs=[row_spec(inner)] * 4
            + [whole(lowers[0].shape)] * 4
            + [row_spec(columns), whole(masks.shape)],
            out_specs=(row_spec(columns), whole((owners, SLOTS + 16, 2 * B * B))),
            scratch_shapes=[
                pltpu.VMEM((4 * (2 * rows + 2 * inner), 128), jnp.bfloat16),
                pltpu.VMEM((owners * SLOTS * 16, 128), jnp.bfloat16),
                pltpu.VMEM((128, 128), jnp.bfloat16),
                pltpu.VMEM((2, 8, 128), jnp.float32),
                pltpu.VMEM((SLOTS, SLOTS * 8), jnp.bfloat16),
            ],
        ),
        compiler_params=pltpu.CompilerParams(vmem_limit_bytes=60 * MIB),
        cost_estimate=pl.CostEstimate(
            flops=2 * rows * inner * 16 * columns, bytes_accessed=12 << 20, transcendentals=0
        ),
        name="block_and_pairs",
    )(base, slot, codes, counts, *couplings, *lowers, diag, masks)


def pole_sum_kernel(weight_ref, parts_ref, out_ref):
    lane = lax.broadcasted_iota(jnp.int32, (1, 128), 1).astype(jnp.float32)
    straight = crossed = None
    for p in range(parts_ref.shape[0]):
        part = parts_ref[p, :SLOTS, :].astype(jnp.float32)
        slot = parts_ref[p, SLOTS:, :].astype(jnp.float32)[:1]
        weight = []
        for c in range(2):
            found = jnp.where(slot == lane, weight_ref[c : c + 1, :128], 0.0) + jnp.where(
                slot == lane + 128.0, weight_ref[c : c + 1, 128:], 0.0
            )
            weight.append(jnp.sum(found, axis=1, keepdims=True))
        a = weight[0] * part
        b = weight[1] * part
        straight = a if straight is None else straight + a
        crossed = b if crossed is None else crossed + b
    half = B * B
    lane = lax.broadcasted_iota(jnp.int32, crossed.shape, 1)
    crossed = pltpu.roll(crossed, half, 1)
    total = (straight + jnp.where(lane < half, -crossed, crossed)).astype(out_ref.dtype)
    for cell in range(out_ref.shape[0]):
        out_ref[cell] = total


def pole_sum_call(weights, parts, copies):
    return pl.pallas_call(
        pole_sum_kernel,
        out_shape=jax.ShapeDtypeStruct((copies, SLOTS, 2 * B * B), jnp.bfloat16),
        in_specs=[pl.BlockSpec(memory_space=pltpu.VMEM)] * 2,
        out_specs=pl.BlockSpec(memory_space=pltpu.VMEM),
        compiler_params=pltpu.CompilerParams(vmem_limit_bytes=6 * MIB),
        name="pole_sum",
    )(weights, parts)


def density_kernel(index_ref, sums_ref, projector_ref, out_ref, sums):
    sums[...] = sums_ref[...].astype(jnp.float32)

    @pl.loop(0, out_ref.shape[0] // 32)
    def _(group):
        first = pl.multiple_of(group * 32, 32)
        for s in range(32):
            q = first + s
            out_ref[pl.ds(q, 1), :] = sums[pl.ds(index_ref[q], 1), :]

    out_ref[...] = out_ref[...] * projector_ref[...]


def density_call(index, sums, projector):
    return pl.pallas_call(
        density_kernel,
        out_shape=jax.ShapeDtypeStruct(projector.shape, jnp.float32),
        in_specs=[pl.BlockSpec(memory_space=pltpu.SMEM)]
        + [pl.BlockSpec(memory_space=pltpu.VMEM)] * 2,
        out_specs=pl.BlockSpec(memory_space=pltpu.VMEM),
        scratch_shapes=[pltpu.VMEM(sums.shape, jnp.float32)],
        compiler_params=pltpu.CompilerParams(vmem_limit_bytes=6 * MIB),
        name="density",
    )(index, sums, projector)


def pair_tables(pair_row, pair_col, row, col, pole, owners):
    row_atoms, col_atoms, trail_atoms = KA // ROWS, KA // COLS, 128 // COLS
    a = pair_row.reshape(owners, -1)
    b = pair_col.reshape(owners, -1)
    in_super = a < KA
    trail = a - KA
    cell = jnp.where(
        in_super,
        (a // row_atoms) * COLS + b // col_atoms,
        (b // row_atoms) * COLS + trail // trail_atoms,
    )
    table_atom = jnp.where(in_super, a % row_atoms, row_atoms + trail % trail_atoms)
    column_atom = jnp.where(in_super, b % col_atoms, b % row_atoms)
    tile, place = column_atom // 16, column_atom % 16
    code = (tile * (row_atoms + trail_atoms) + table_atom) * 16 + place
    pairs = a.shape[1]
    place = jnp.arange(pairs, dtype=jnp.int32)
    earlier = place[:, None] < place[None, :]
    mine = cell == row * COLS + col
    rank = jnp.dot(
        mine.astype(jnp.bfloat16),
        earlier.astype(jnp.bfloat16),
        preferred_element_type=jnp.float32,
    ).astype(jnp.int32)
    slot = jnp.where(mine, rank, -1)
    hit = slot[:, None, :] == jnp.arange(SLOTS, dtype=jnp.int32)[None, :, None]
    codes = jnp.sum(jnp.where(hit, code[:, None, :], 0), axis=2).reshape(owners * SLOTS)
    own_cell = lax.dynamic_index_in_dim(cell, pole, 0, keepdims=False)
    same = (own_cell[:, None] == own_cell[None, :]) & earlier
    index = own_cell * SLOTS + jnp.sum(same.astype(jnp.int32), axis=0)
    counts = jnp.sum(mine.astype(jnp.int32), axis=1)
    return codes, counts, index


def local(
    inverse_trail, lower_t, diag_inverse, pole_weight, pole_slot, pair_row, pair_col, projector
):
    row = lax.axis_index("row")
    col = lax.axis_index("col")
    pole = lax.axis_index(POLE)
    poles = lax.axis_size(POLE)
    base = ((row - col + COLS) % COLS).astype(jnp.int32).reshape(1)

    trail = parts_apart(inverse_trail[0])
    lower = parts_apart(lower_t[0])
    lower, trail = lax.optimization_barrier((lower, trail))

    trails = [trail] + [lax.ppermute(trail, "row", ring(e, ROWS)) for e in range(1, ROWS)]
    lefts = [lax.ppermute(lower, ("row", "col"), to_process_rows(d)) for d in range(COLS)]

    codes, counts, index = pair_tables(pair_row, pair_col, row, col, pole, poles)
    diag = parts_apart(diag_inverse[0])
    wide_projector = jnp.concatenate([projector, projector], axis=1).astype(jnp.float32)
    masks = (
        jnp.arange(16, dtype=jnp.int32)[:, None, None]
        == jnp.broadcast_to(jnp.arange(128, dtype=jnp.int32) // B, (16, 128))[None]
    ).astype(jnp.bfloat16)

    coupling = coupling_call(base, lefts, trails)
    lower_late, coupling = lax.optimization_barrier((lower, coupling))
    couplings = [coupling] + [
        lax.ppermute(coupling, "col", ring(d, COLS)) for d in range(1, COLS)
    ]
    lowers = [lower] + [lax.ppermute(lower_late, "row", ring(e, ROWS)) for e in range(1, ROWS)]

    block, pairs = block_call(
        base, pole_slot, codes, counts, couplings, lowers, diag, masks
    )
    out = block.transpose(1, 0, 2)[None]

    parts = lax.all_to_all(pairs, POLE, 0, 0, tiled=True)
    cells = ROWS * COLS
    summed = pole_sum_call(pole_weight.T, parts, cells)
    everywhere = lax.all_to_all(summed, ("row", "col"), 0, 0, tiled=True)
    density = density_call(index, everywhere.reshape(cells * SLOTS, 2 * B * B), wide_projector)
    return (out, density)


def solution(mesh):
    split = Mesh(
        mesh.devices.reshape(8, 2, mesh.shape["row"], mesh.shape["col"]),
        ("pole_0", "pole_1", "row", "col"),
    )
    in_specs = (
        P(POLE, "row", None, "col"),
        P(POLE, "col", None, "row"),
        P(POLE, "row", None, "col"),
        P(),
        P(POLE),
        P(),
        P(),
        P(POLE, None),
    )
    out_specs = (P(POLE, "row", None, "col"), P(POLE, None))
    return jax.shard_map(local, mesh=split, in_specs=in_specs, out_specs=out_specs, check_vma=False)
```

```python
import jax
import jax.numpy as jnp
from jax import lax
from jax.experimental import pallas as pl
from jax.experimental.pallas import tpu as pltpu
from jax.sharding import Mesh
from jax.sharding import PartitionSpec as P

B = 8
KA = 256
POLE = ("pole_0", "pole_1")
ROWS = 4
COLS = 4
SLOTS = 64
GROUP = 16
MIB = 1 << 20


def ring(shift, peers):
    return [(i, (i + shift) % peers) for i in range(peers)]


def to_process_rows(shift):
    return [
        (k * COLS + x, x * COLS + (x + k + shift) % COLS)
        for k in range(ROWS)
        for x in range(COLS)
    ]


def parts_apart(raw):
    return raw.transpose(1, 0, 2)


def whole(shape):
    return pl.BlockSpec(shape, lambda *_: (0,) * len(shape))


def product(left, right, dim):
    return lax.dot_general(
        left, right, (((1,), (dim,)), ((), ())), preferred_element_type=jnp.float32
    )


def complex_product(lefts, rights, dim, order):
    left = jnp.concatenate([x[...].reshape(-1, x.shape[2]) for x in lefts], axis=1)
    real = jnp.concatenate([rights[e][0] for e in order], axis=dim)
    imag = jnp.concatenate([rights[e][1] for e in order], axis=dim)
    half = left.shape[0] // 2
    u = product(left, real, dim)
    v = product(left, imag, dim)
    return u[:half] - v[half:], u[half:] + v[:half]


def by_atom(re, im):
    rows, columns = re.shape
    pair = [x.reshape(rows // B, B, columns) for x in (re, im)]
    return jnp.stack(pair, axis=1).reshape(2 * rows, columns).astype(jnp.bfloat16)


def coupling_kernel(base_ref, l0, l1, l2, l3, t0, t1, t2, t3, c_ref):
    def run(order):
        re, im = complex_product((l0, l1, l2, l3), (t0, t1, t2, t3), 0, order)
        c_ref[0] = (-re).astype(jnp.bfloat16)
        c_ref[1] = (-im).astype(jnp.bfloat16)

    for base in range(ROWS):

        @pl.when(base_ref[0] == base)
        def _():
            run([(base + d) % ROWS for d in range(ROWS)])


def coupling_call(base, lefts, trails):
    _, rows, inner = lefts[0].shape
    columns = trails[0].shape[2]
    return pl.pallas_call(
        coupling_kernel,
        out_shape=jax.ShapeDtypeStruct((2, rows, columns), jnp.bfloat16),
        grid_spec=pltpu.PrefetchScalarGridSpec(
            num_scalar_prefetch=1,
            grid=(1,),
            in_specs=[whole(lefts[0].shape)] * 4 + [whole(trails[0].shape)] * 4,
            out_specs=whole((2, rows, columns)),
        ),
        compiler_params=pltpu.CompilerParams(vmem_limit_bytes=14 * MIB),
        cost_estimate=pl.CostEstimate(
            flops=2 * rows * inner * 16 * columns, bytes_accessed=3 << 20, transcendentals=0
        ),
        name="coupling",
    )(base, *lefts, *trails)


def take_pairs(codes_ref, counts_ref, mask_ref, pairs_ref, table, lanes, spread, keep, fold):
    owners = pairs_ref.shape[0]

    @pl.loop(0, owners * SLOTS // GROUP)
    def _(group):
        first = group * GROUP
        to = pl.multiple_of(first * 16, GROUP * 16)
        used = counts_ref[first // SLOTS] > first % SLOTS

        @pl.when(used)
        def _():
            for s in range(GROUP):
                code = codes_ref[first + s]
                found = table[pl.ds(pl.multiple_of(code & ~15, 16), 16), :]
                lanes[pl.ds(to + s * 16, 16), :] = found * mask_ref[code & 15]

        @pl.when(jnp.logical_not(used))
        def _():
            lanes[pl.ds(to, GROUP * 16), :] = jnp.zeros((GROUP * 16, 128), jnp.bfloat16)

    many = 4

    @pl.loop(0, owners // many)
    def _(chunk):
        rows = many * SLOTS * 16
        wide = product(lanes[pl.ds(pl.multiple_of(chunk * rows, rows), rows), :], spread[...], 0)
        wide = wide.reshape(many * SLOTS, 2, 8, 2 * B * B) * keep[...][None]
        wide = (wide[:, 0] + wide[:, 1]).reshape(many, SLOTS * 8, 2 * B * B).astype(jnp.bfloat16)
        for o in range(many):
            pairs_ref[chunk * many + o, :SLOTS, :] = product(fold[...], wide[o], 0).astype(
                jnp.bfloat16
            )


def block_kernel(
    base_ref, slot_ref, codes_ref, counts_ref, *refs
):
    first_half, second_half, lowers = refs[:4], refs[4:8], refs[8:12]
    diag_ref, mask_ref, out_ref, pairs_ref, table, lanes, spread, keep, fold = refs[12:]
    step = pl.program_id(0)
    last = pl.num_programs(0) - 1
    tile = out_ref.shape[1]
    per_tile = table.shape[0] // 4
    trail_rows = 2 * refs[0].shape[2]
    super_rows = per_tile - trail_rows

    @pl.when(step == 0)
    def _():
        lane = lax.broadcasted_iota(jnp.int32, (128, 128), 1)
        row = lax.broadcasted_iota(jnp.int32, (128, 128), 0)
        spread[...] = jnp.where(row % 8 == lane % 8, 1.0, 0.0).astype(jnp.bfloat16)
        part = lax.broadcasted_iota(jnp.int32, (2, 8, 128), 0)
        row = lax.broadcasted_iota(jnp.int32, (2, 8, 128), 1)
        lane = lax.broadcasted_iota(jnp.int32, (2, 8, 128), 2)
        keep[...] = jnp.where(lane // 8 == part * 8 + row, 1.0, 0.0)
        row = lax.broadcasted_iota(jnp.int32, fold.shape, 0)
        lane = lax.broadcasted_iota(jnp.int32, fold.shape, 1)
        fold[...] = jnp.where(lane // 8 == row, 1.0, 0.0).astype(jnp.bfloat16)
        slot = jnp.full((16, 128), slot_ref[0], jnp.int32).astype(jnp.float32)
        for owner in range(pairs_ref.shape[0]):
            pairs_ref[owner, SLOTS:, :] = slot.astype(jnp.bfloat16)

    def run(order, couplings):
        re, im = complex_product(couplings, lowers, 1, order)
        re = diag_ref[0].astype(jnp.float32) - re
        im = diag_ref[1].astype(jnp.float32) - im
        out_ref[0] = re.astype(jnp.bfloat16)
        out_ref[1] = im.astype(jnp.bfloat16)
        rows = by_atom(re, im)
        for t in range(4):
            first = pl.multiple_of(t * per_tile + step * 2 * tile, 2 * tile)
            table[pl.ds(first, 2 * tile), :] = rows[:, t * 128 : t * 128 + 128]
        own = [couplings[0][part].astype(jnp.float32).T for part in range(2)]
        rows = by_atom(own[0], own[1])
        for t in range(tile // 128):
            first = pl.multiple_of((step * (tile // 128) + t) * per_tile + super_rows, trail_rows)
            table[pl.ds(first, trail_rows), :] = rows[:, t * 128 : t * 128 + 128]

    for base in range(ROWS):
        for half, couplings in enumerate((first_half, second_half)):

            @pl.when((base_ref[0] == base) & (step == half))
            def _():
                run([(base + d) % ROWS for d in range(ROWS)], couplings)

    @pl.when(step == last)
    def _():
        take_pairs(codes_ref, counts_ref, mask_ref, pairs_ref, table, lanes, spread, keep, fold)


def block_call(base, slot, codes, counts, couplings, lowers, diag, masks):
    _, rows, columns = diag.shape
    inner = couplings[0].shape[2]
    owners = codes.shape[0] // SLOTS
    tile = couplings[0].shape[1]
    row_spec = lambda last: pl.BlockSpec((2, tile, last), lambda i, *_: (0, i, 0))
    return pl.pallas_call(
        block_kernel,
        out_shape=(
            jax.ShapeDtypeStruct((2, rows, columns), jnp.bfloat16),
            jax.ShapeDtypeStruct((owners, SLOTS + 16, 2 * B * B), jnp.bfloat16),
        ),
        grid_spec=pltpu.PrefetchScalarGridSpec(
            num_scalar_prefetch=4,
            grid=(rows // tile,),
            in_specs=[whole(couplings[0].shape)] * 8
            + [whole(lowers[0].shape)] * 4
            + [row_spec(columns), whole(masks.shape)],
            out_specs=(row_spec(columns), whole((owners, SLOTS + 16, 2 * B * B))),
            scratch_shapes=[
                pltpu.VMEM((4 * (2 * rows + 2 * inner), 128), jnp.bfloat16),
                pltpu.VMEM((owners * SLOTS * 16, 128), jnp.bfloat16),
                pltpu.VMEM((128, 128), jnp.bfloat16),
                pltpu.VMEM((2, 8, 128), jnp.float32),
                pltpu.VMEM((SLOTS, SLOTS * 8), jnp.bfloat16),
            ],
        ),
        compiler_params=pltpu.CompilerParams(vmem_limit_bytes=60 * MIB),
        cost_estimate=pl.CostEstimate(
            flops=2 * rows * inner * 16 * columns, bytes_accessed=12 << 20, transcendentals=0
        ),
        name="block_and_pairs",
    )(base, slot, codes, counts, *couplings, *lowers, diag, masks)


def pole_sum_kernel(weight_ref, parts_ref, out_ref):
    lane = lax.broadcasted_iota(jnp.int32, (1, 128), 1).astype(jnp.float32)
    straight = crossed = None
    for p in range(parts_ref.shape[0]):
        part = parts_ref[p, :SLOTS, :].astype(jnp.float32)
        slot = parts_ref[p, SLOTS:, :].astype(jnp.float32)[:1]
        weight = []
        for c in range(2):
            found = jnp.where(slot == lane, weight_ref[c : c + 1, :128], 0.0) + jnp.where(
                slot == lane + 128.0, weight_ref[c : c + 1, 128:], 0.0
            )
            weight.append(jnp.sum(found, axis=1, keepdims=True))
        a = weight[0] * part
        b = weight[1] * part
        straight = a if straight is None else straight + a
        crossed = b if crossed is None else crossed + b
    half = B * B
    lane = lax.broadcasted_iota(jnp.int32, crossed.shape, 1)
    crossed = pltpu.roll(crossed, half, 1)
    total = (straight + jnp.where(lane < half, -crossed, crossed)).astype(out_ref.dtype)
    for cell in range(out_ref.shape[0]):
        out_ref[cell] = total


def pole_sum_call(weights, parts, copies):
    return pl.pallas_call(
        pole_sum_kernel,
        out_shape=jax.ShapeDtypeStruct((copies, SLOTS, 2 * B * B), jnp.bfloat16),
        in_specs=[pl.BlockSpec(memory_space=pltpu.VMEM)] * 2,
        out_specs=pl.BlockSpec(memory_space=pltpu.VMEM),
        compiler_params=pltpu.CompilerParams(vmem_limit_bytes=6 * MIB),
        name="pole_sum",
    )(weights, parts)


def density_kernel(index_ref, sums_ref, projector_ref, out_ref, sums):
    sums[...] = sums_ref[...].astype(jnp.float32)

    @pl.loop(0, out_ref.shape[0] // 32)
    def _(group):
        first = pl.multiple_of(group * 32, 32)
        for s in range(32):
            q = first + s
            out_ref[pl.ds(q, 1), :] = sums[pl.ds(index_ref[q], 1), :]

    out_ref[...] = out_ref[...] * projector_ref[...]


def density_call(index, sums, projector):
    return pl.pallas_call(
        density_kernel,
        out_shape=jax.ShapeDtypeStruct(projector.shape, jnp.float32),
        in_specs=[pl.BlockSpec(memory_space=pltpu.SMEM)]
        + [pl.BlockSpec(memory_space=pltpu.VMEM)] * 2,
        out_specs=pl.BlockSpec(memory_space=pltpu.VMEM),
        scratch_shapes=[pltpu.VMEM(sums.shape, jnp.float32)],
        compiler_params=pltpu.CompilerParams(vmem_limit_bytes=6 * MIB),
        name="density",
    )(index, sums, projector)


def pair_tables(pair_row, pair_col, row, col, pole, owners):
    row_atoms, col_atoms, trail_atoms = KA // ROWS, KA // COLS, 128 // COLS
    a = pair_row.reshape(owners, -1)
    b = pair_col.reshape(owners, -1)
    in_super = a < KA
    trail = a - KA
    cell = jnp.where(
        in_super,
        (a // row_atoms) * COLS + b // col_atoms,
        (b // row_atoms) * COLS + trail // trail_atoms,
    )
    table_atom = jnp.where(in_super, a % row_atoms, row_atoms + trail % trail_atoms)
    column_atom = jnp.where(in_super, b % col_atoms, b % row_atoms)
    tile, place = column_atom // 16, column_atom % 16
    code = (tile * (row_atoms + trail_atoms) + table_atom) * 16 + place
    pairs = a.shape[1]
    place = jnp.arange(pairs, dtype=jnp.int32)
    earlier = place[:, None] < place[None, :]
    mine = cell == row * COLS + col
    rank = jnp.dot(
        mine.astype(jnp.bfloat16),
        earlier.astype(jnp.bfloat16),
        preferred_element_type=jnp.float32,
    ).astype(jnp.int32)
    slot = jnp.where(mine, rank, -1)
    hit = slot[:, None, :] == jnp.arange(SLOTS, dtype=jnp.int32)[None, :, None]
    codes = jnp.sum(jnp.where(hit, code[:, None, :], 0), axis=2).reshape(owners * SLOTS)
    own_cell = lax.dynamic_index_in_dim(cell, pole, 0, keepdims=False)
    same = (own_cell[:, None] == own_cell[None, :]) & earlier
    index = own_cell * SLOTS + jnp.sum(same.astype(jnp.int32), axis=0)
    counts = jnp.sum(mine.astype(jnp.int32), axis=1)
    return codes, counts, index


def local(
    inverse_trail, lower_t, diag_inverse, pole_weight, pole_slot, pair_row, pair_col, projector
):
    row = lax.axis_index("row")
    col = lax.axis_index("col")
    pole = lax.axis_index(POLE)
    poles = lax.axis_size(POLE)
    base = ((row - col + COLS) % COLS).astype(jnp.int32).reshape(1)

    trail = parts_apart(inverse_trail[0])
    lower = parts_apart(lower_t[0])
    half = lower.shape[1] // 2
    halves = [parts_apart(lower_t[0, :half]), parts_apart(lower_t[0, half:])]
    lower, trail, halves = lax.optimization_barrier((lower, trail, halves))
    pair_axes = ("row", "col")

    trails = [trail] + [lax.ppermute(trail, "row", ring(e, ROWS)) for e in range(1, ROWS)]
    first = [lax.ppermute(halves[0], pair_axes, to_process_rows(e)) for e in range(COLS)]
    second_half, _ = lax.optimization_barrier((halves[1], first[0]))
    second = [lax.ppermute(second_half, pair_axes, to_process_rows(e)) for e in range(COLS)]

    codes, counts, index = pair_tables(pair_row, pair_col, row, col, pole, poles)
    diag = parts_apart(diag_inverse[0])
    wide_projector = jnp.concatenate([projector, projector], axis=1).astype(jnp.float32)
    masks = (
        jnp.arange(16, dtype=jnp.int32)[:, None, None]
        == jnp.broadcast_to(jnp.arange(128, dtype=jnp.int32) // B, (16, 128))[None]
    ).astype(jnp.bfloat16)

    trail_base = ((2 * row - col + COLS) % COLS).astype(jnp.int32).reshape(1)
    couplings = []
    for lefts in (first, second):
        coupling = coupling_call(trail_base, lefts, trails)
        if not couplings:
            lower_late, coupling = lax.optimization_barrier((lower, coupling))
        couplings += [coupling] + [
            lax.ppermute(coupling, "col", ring(d, COLS)) for d in range(1, COLS)
        ]
    lowers = [lower] + [lax.ppermute(lower_late, "row", ring(e, ROWS)) for e in range(1, ROWS)]

    block, pairs = block_call(
        base, pole_slot, codes, counts, couplings, lowers, diag, masks
    )
    out = block.transpose(1, 0, 2)[None]

    parts = lax.all_to_all(pairs, POLE, 0, 0, tiled=True)
    cells = ROWS * COLS
    summed = pole_sum_call(pole_weight.T, parts, cells)
    everywhere = lax.all_to_all(summed, ("row", "col"), 0, 0, tiled=True)
    density = density_call(index, everywhere.reshape(cells * SLOTS, 2 * B * B), wide_projector)
    return (out, density)


def solution(mesh):
    split = Mesh(
        mesh.devices.reshape(8, 2, mesh.shape["row"], mesh.shape["col"]),
        ("pole_0", "pole_1", "row", "col"),
    )
    in_specs = (
        P(POLE, "row", None, "col"),
        P(POLE, "col", None, "row"),
        P(POLE, "row", None, "col"),
        P(),
        P(POLE),
        P(),
        P(),
        P(POLE, None),
    )
    out_specs = (P(POLE, "row", None, "col"), P(POLE, None))
    return jax.shard_map(local, mesh=split, in_specs=in_specs, out_specs=out_specs, check_vma=False)
```

```python
import jax
import jax.numpy as jnp
from jax import lax
from jax.experimental import pallas as pl
from jax.experimental.pallas import tpu as pltpu
from jax.sharding import Mesh
from jax.sharding import PartitionSpec as P

B = 8
KA = 256
POLE = ("pole_0", "pole_1")
ROWS = 4
COLS = 4
SLOTS = 64
GROUP = 16
MIB = 1 << 20


def ring(shift, peers):
    return [(i, (i + shift) % peers) for i in range(peers)]


def to_process_rows(shift):
    return [
        (k * COLS + x, x * COLS + (x + k + shift) % COLS)
        for k in range(ROWS)
        for x in range(COLS)
    ]


def parts_apart(raw):
    return raw.transpose(1, 0, 2)


def whole(shape):
    return pl.BlockSpec(shape, lambda *_: (0,) * len(shape))


def product(left, right, dim):
    return lax.dot_general(
        left, right, (((1,), (dim,)), ((), ())), preferred_element_type=jnp.float32
    )


def complex_product(lefts, rights, dim, order):
    left = jnp.concatenate([x[...].reshape(-1, x.shape[2]) for x in lefts], axis=1)
    real = jnp.concatenate([rights[e][0] for e in order], axis=dim)
    imag = jnp.concatenate([rights[e][1] for e in order], axis=dim)
    half = left.shape[0] // 2
    u = product(left, real, dim)
    v = product(left, imag, dim)
    return u[:half] - v[half:], u[half:] + v[:half]


def by_atom(re, im):
    rows, columns = re.shape
    pair = [x.reshape(rows // B, B, columns) for x in (re, im)]
    return jnp.stack(pair, axis=1).reshape(2 * rows, columns).astype(jnp.bfloat16)


def coupling_kernel(base_ref, l0, l1, l2, l3, t0, t1, t2, t3, c_ref):
    def run(order):
        re, im = complex_product((l0, l1, l2, l3), (t0, t1, t2, t3), 0, order)
        c_ref[0] = (-re).astype(jnp.bfloat16)
        c_ref[1] = (-im).astype(jnp.bfloat16)

    for base in range(ROWS):

        @pl.when(base_ref[0] == base)
        def _():
            run([(base + d) % ROWS for d in range(ROWS)])


def coupling_call(base, lefts, trails):
    _, rows, inner = lefts[0].shape
    columns = trails[0].shape[2]
    return pl.pallas_call(
        coupling_kernel,
        out_shape=jax.ShapeDtypeStruct((2, rows, columns), jnp.bfloat16),
        grid_spec=pltpu.PrefetchScalarGridSpec(
            num_scalar_prefetch=1,
            grid=(1,),
            in_specs=[whole(lefts[0].shape)] * 4 + [whole(trails[0].shape)] * 4,
            out_specs=whole((2, rows, columns)),
        ),
        compiler_params=pltpu.CompilerParams(vmem_limit_bytes=14 * MIB),
        cost_estimate=pl.CostEstimate(
            flops=2 * rows * inner * 16 * columns, bytes_accessed=3 << 20, transcendentals=0
        ),
        name="coupling",
    )(base, *lefts, *trails)


def take_pairs(codes_ref, counts_ref, mask_ref, pairs_ref, table, lanes, spread, keep, fold):
    owners = pairs_ref.shape[0]

    @pl.loop(0, owners * SLOTS // GROUP)
    def _(group):
        first = group * GROUP
        to = pl.multiple_of(first * 16, GROUP * 16)
        used = counts_ref[first // SLOTS] > first % SLOTS

        @pl.when(used)
        def _():
            for s in range(GROUP):
                code = codes_ref[first + s]
                found = table[pl.ds(pl.multiple_of(code & ~15, 16), 16), :]
                lanes[pl.ds(to + s * 16, 16), :] = found * mask_ref[code & 15]

        @pl.when(jnp.logical_not(used))
        def _():
            lanes[pl.ds(to, GROUP * 16), :] = jnp.zeros((GROUP * 16, 128), jnp.bfloat16)

    many = 4

    @pl.loop(0, owners // many)
    def _(chunk):
        rows = many * SLOTS * 16
        wide = product(lanes[pl.ds(pl.multiple_of(chunk * rows, rows), rows), :], spread[...], 0)
        wide = wide.reshape(many * SLOTS, 2, 8, 2 * B * B) * keep[...][None]
        wide = (wide[:, 0] + wide[:, 1]).reshape(many, SLOTS * 8, 2 * B * B).astype(jnp.bfloat16)
        for o in range(many):
            pairs_ref[chunk * many + o, :SLOTS, :] = product(fold[...], wide[o], 0).astype(
                jnp.bfloat16
            )


def block_kernel(
    base_ref, slot_ref, codes_ref, counts_ref, *refs
):
    first_half, second_half, lowers = refs[:4], refs[4:8], refs[8:12]
    diag_ref, mask_ref, out_ref, pairs_ref, table, lanes, spread, keep, fold = refs[12:]
    step = pl.program_id(0)
    last = pl.num_programs(0) - 1
    tile = out_ref.shape[1]
    per_tile = table.shape[0] // 4
    trail_rows = 2 * refs[0].shape[2]
    super_rows = per_tile - trail_rows

    @pl.when(step == 0)
    def _():
        lane = lax.broadcasted_iota(jnp.int32, (128, 128), 1)
        row = lax.broadcasted_iota(jnp.int32, (128, 128), 0)
        spread[...] = jnp.where(row % 8 == lane % 8, 1.0, 0.0).astype(jnp.bfloat16)
        part = lax.broadcasted_iota(jnp.int32, (2, 8, 128), 0)
        row = lax.broadcasted_iota(jnp.int32, (2, 8, 128), 1)
        lane = lax.broadcasted_iota(jnp.int32, (2, 8, 128), 2)
        keep[...] = jnp.where(lane // 8 == part * 8 + row, 1.0, 0.0)
        row = lax.broadcasted_iota(jnp.int32, fold.shape, 0)
        lane = lax.broadcasted_iota(jnp.int32, fold.shape, 1)
        fold[...] = jnp.where(lane // 8 == row, 1.0, 0.0).astype(jnp.bfloat16)
        slot = jnp.full((16, 128), slot_ref[0], jnp.int32).astype(jnp.float32)
        for owner in range(pairs_ref.shape[0]):
            pairs_ref[owner, SLOTS:, :] = slot.astype(jnp.bfloat16)

    def run(order, couplings):
        re, im = complex_product(couplings, lowers, 1, order)
        re = diag_ref[0].astype(jnp.float32) - re
        im = diag_ref[1].astype(jnp.float32) - im
        out_ref[0] = re.astype(jnp.bfloat16)
        out_ref[1] = im.astype(jnp.bfloat16)
        rows = by_atom(re, im)
        for t in range(4):
            first = pl.multiple_of(t * per_tile + step * 2 * tile, 2 * tile)
            table[pl.ds(first, 2 * tile), :] = rows[:, t * 128 : t * 128 + 128]
        own = [couplings[0][part].astype(jnp.float32).T for part in range(2)]
        rows = by_atom(own[0], own[1])
        for t in range(tile // 128):
            first = pl.multiple_of((step * (tile // 128) + t) * per_tile + super_rows, trail_rows)
            table[pl.ds(first, trail_rows), :] = rows[:, t * 128 : t * 128 + 128]

    for base in range(ROWS):
        for half, couplings in enumerate((first_half, second_half)):

            @pl.when((base_ref[0] == base) & (step == half))
            def _():
                run([(base + d) % ROWS for d in range(ROWS)], couplings)

    @pl.when(step == last)
    def _():
        take_pairs(codes_ref, counts_ref, mask_ref, pairs_ref, table, lanes, spread, keep, fold)


def block_call(base, slot, codes, counts, couplings, lowers, diag, masks):
    _, rows, columns = diag.shape
    inner = couplings[0].shape[2]
    owners = codes.shape[0] // SLOTS
    tile = couplings[0].shape[1]
    row_spec = lambda last: pl.BlockSpec((2, tile, last), lambda i, *_: (0, i, 0))
    return pl.pallas_call(
        block_kernel,
        out_shape=(
            jax.ShapeDtypeStruct((2, rows, columns), jnp.bfloat16),
            jax.ShapeDtypeStruct((owners, SLOTS + 16, 2 * B * B), jnp.bfloat16),
        ),
        grid_spec=pltpu.PrefetchScalarGridSpec(
            num_scalar_prefetch=4,
            grid=(rows // tile,),
            in_specs=[whole(couplings[0].shape)] * 8
            + [whole(lowers[0].shape)] * 4
            + [row_spec(columns), whole(masks.shape)],
            out_specs=(row_spec(columns), whole((owners, SLOTS + 16, 2 * B * B))),
            scratch_shapes=[
                pltpu.VMEM((4 * (2 * rows + 2 * inner), 128), jnp.bfloat16),
                pltpu.VMEM((owners * SLOTS * 16, 128), jnp.bfloat16),
                pltpu.VMEM((128, 128), jnp.bfloat16),
                pltpu.VMEM((2, 8, 128), jnp.float32),
                pltpu.VMEM((SLOTS, SLOTS * 8), jnp.bfloat16),
            ],
        ),
        compiler_params=pltpu.CompilerParams(vmem_limit_bytes=52 * MIB),
        cost_estimate=pl.CostEstimate(
            flops=2 * rows * inner * 16 * columns, bytes_accessed=12 << 20, transcendentals=0
        ),
        name="block_and_pairs",
    )(base, slot, codes, counts, *couplings, *lowers, diag, masks)


def pole_sum_kernel(weight_ref, parts_ref, out_ref):
    lane = lax.broadcasted_iota(jnp.int32, (1, 128), 1).astype(jnp.float32)
    straight = crossed = None
    for p in range(parts_ref.shape[0]):
        part = parts_ref[p, :SLOTS, :].astype(jnp.float32)
        slot = parts_ref[p, SLOTS:, :].astype(jnp.float32)[:1]
        weight = []
        for c in range(2):
            found = jnp.where(slot == lane, weight_ref[c : c + 1, :128], 0.0) + jnp.where(
                slot == lane + 128.0, weight_ref[c : c + 1, 128:], 0.0
            )
            weight.append(jnp.sum(found, axis=1, keepdims=True))
        a = weight[0] * part
        b = weight[1] * part
        straight = a if straight is None else straight + a
        crossed = b if crossed is None else crossed + b
    half = B * B
    lane = lax.broadcasted_iota(jnp.int32, crossed.shape, 1)
    crossed = pltpu.roll(crossed, half, 1)
    total = (straight + jnp.where(lane < half, -crossed, crossed)).astype(out_ref.dtype)
    for cell in range(out_ref.shape[0]):
        out_ref[cell] = total


def pole_sum_call(weights, parts, copies):
    return pl.pallas_call(
        pole_sum_kernel,
        out_shape=jax.ShapeDtypeStruct((copies, SLOTS, 2 * B * B), jnp.bfloat16),
        in_specs=[pl.BlockSpec(memory_space=pltpu.VMEM)] * 2,
        out_specs=pl.BlockSpec(memory_space=pltpu.VMEM),
        compiler_params=pltpu.CompilerParams(vmem_limit_bytes=6 * MIB),
        name="pole_sum",
    )(weights, parts)


def density_kernel(index_ref, sums_ref, projector_ref, out_ref, sums):
    sums[...] = sums_ref[...].astype(jnp.float32)

    @pl.loop(0, out_ref.shape[0] // 32)
    def _(group):
        first = pl.multiple_of(group * 32, 32)
        for s in range(32):
            q = first + s
            out_ref[pl.ds(q, 1), :] = sums[pl.ds(index_ref[q], 1), :]

    out_ref[...] = out_ref[...] * projector_ref[...]


def density_call(index, sums, projector):
    return pl.pallas_call(
        density_kernel,
        out_shape=jax.ShapeDtypeStruct(projector.shape, jnp.float32),
        in_specs=[pl.BlockSpec(memory_space=pltpu.SMEM)]
        + [pl.BlockSpec(memory_space=pltpu.VMEM)] * 2,
        out_specs=pl.BlockSpec(memory_space=pltpu.VMEM),
        scratch_shapes=[pltpu.VMEM(sums.shape, jnp.float32)],
        compiler_params=pltpu.CompilerParams(vmem_limit_bytes=6 * MIB),
        name="density",
    )(index, sums, projector)


def pair_tables(pair_row, pair_col, row, col, pole, owners):
    row_atoms, col_atoms, trail_atoms = KA // ROWS, KA // COLS, 128 // COLS
    a = pair_row.reshape(owners, -1)
    b = pair_col.reshape(owners, -1)
    in_super = a < KA
    trail = a - KA
    cell = jnp.where(
        in_super,
        (a // row_atoms) * COLS + b // col_atoms,
        (b // row_atoms) * COLS + trail // trail_atoms,
    )
    table_atom = jnp.where(in_super, a % row_atoms, row_atoms + trail % trail_atoms)
    column_atom = jnp.where(in_super, b % col_atoms, b % row_atoms)
    tile, place = column_atom // 16, column_atom % 16
    code = (tile * (row_atoms + trail_atoms) + table_atom) * 16 + place
    pairs = a.shape[1]
    place = jnp.arange(pairs, dtype=jnp.int32)
    earlier = place[:, None] < place[None, :]
    mine = cell == row * COLS + col
    rank = jnp.dot(
        mine.astype(jnp.bfloat16),
        earlier.astype(jnp.bfloat16),
        preferred_element_type=jnp.float32,
    ).astype(jnp.int32)
    slot = jnp.where(mine, rank, -1)
    hit = slot[:, None, :] == jnp.arange(SLOTS, dtype=jnp.int32)[None, :, None]
    codes = jnp.sum(jnp.where(hit, code[:, None, :], 0), axis=2).reshape(owners * SLOTS)
    own_cell = lax.dynamic_index_in_dim(cell, pole, 0, keepdims=False)
    same = (own_cell[:, None] == own_cell[None, :]) & earlier
    index = own_cell * SLOTS + jnp.sum(same.astype(jnp.int32), axis=0)
    counts = jnp.sum(mine.astype(jnp.int32), axis=1)
    return codes, counts, index


def local(
    inverse_trail, lower_t, diag_inverse, pole_weight, pole_slot, pair_row, pair_col, projector
):
    row = lax.axis_index("row")
    col = lax.axis_index("col")
    pole = lax.axis_index(POLE)
    poles = lax.axis_size(POLE)
    base = ((row - col + COLS) % COLS).astype(jnp.int32).reshape(1)

    trail = parts_apart(inverse_trail[0])
    lower = parts_apart(lower_t[0])
    half = lower.shape[1] // 2
    halves = [parts_apart(lower_t[0, :half]), parts_apart(lower_t[0, half:])]
    lower, trail, halves = lax.optimization_barrier((lower, trail, halves))
    pair_axes = ("row", "col")

    trails = [trail] + [lax.ppermute(trail, "row", ring(e, ROWS)) for e in range(1, ROWS)]
    first = [lax.ppermute(halves[0], pair_axes, to_process_rows(e)) for e in range(COLS)]
    second_half, _ = lax.optimization_barrier((halves[1], first[0]))
    second = [lax.ppermute(second_half, pair_axes, to_process_rows(e)) for e in range(COLS)]

    codes, counts, index = pair_tables(pair_row, pair_col, row, col, pole, poles)
    diag = parts_apart(diag_inverse[0])
    wide_projector = jnp.concatenate([projector, projector], axis=1).astype(jnp.float32)
    masks = (
        jnp.arange(16, dtype=jnp.int32)[:, None, None]
        == jnp.broadcast_to(jnp.arange(128, dtype=jnp.int32) // B, (16, 128))[None]
    ).astype(jnp.bfloat16)

    trail_base = ((2 * row - col + COLS) % COLS).astype(jnp.int32).reshape(1)
    couplings = []
    for lefts in (first, second):
        coupling = coupling_call(trail_base, lefts, trails)
        if not couplings:
            lower_late, coupling = lax.optimization_barrier((lower, coupling))
        couplings += [coupling] + [
            lax.ppermute(coupling, "col", ring(d, COLS)) for d in range(1, COLS)
        ]
    lowers = [lower] + [lax.ppermute(lower_late, "row", ring(e, ROWS)) for e in range(1, ROWS)]

    block, pairs = block_call(
        base, pole_slot, codes, counts, couplings, lowers, diag, masks
    )
    out = block.transpose(1, 0, 2)[None]

    parts = lax.all_to_all(pairs, POLE, 0, 0, tiled=True)
    cells = ROWS * COLS
    summed = pole_sum_call(pole_weight.T, parts, cells)
    everywhere = lax.all_to_all(summed, ("row", "col"), 0, 0, tiled=True)
    density = density_call(index, everywhere.reshape(cells * SLOTS, 2 * B * B), wide_projector)
    return (out, density)


def solution(mesh):
    split = Mesh(
        mesh.devices.reshape(8, 2, mesh.shape["row"], mesh.shape["col"]),
        ("pole_0", "pole_1", "row", "col"),
    )
    in_specs = (
        P(POLE, "row", None, "col"),
        P(POLE, "col", None, "row"),
        P(POLE, "row", None, "col"),
        P(),
        P(POLE),
        P(),
        P(),
        P(POLE, None),
    )
    out_specs = (P(POLE, "row", None, "col"), P(POLE, None))
    return jax.shard_map(local, mesh=split, in_specs=in_specs, out_specs=out_specs, check_vma=False)
```

```python
import jax
import jax.numpy as jnp
from jax import lax
from jax.experimental import pallas as pl
from jax.experimental.pallas import tpu as pltpu
from jax.sharding import Mesh
from jax.sharding import PartitionSpec as P

B = 8
KA = 256
POLE = ("pole_0", "pole_1")
ROWS = 4
COLS = 4
SLOTS = 64
GROUP = 16
MIB = 1 << 20


def ring(shift, peers):
    return [(i, (i + shift) % peers) for i in range(peers)]


def to_process_rows(shift):
    return [
        (k * COLS + x, x * COLS + (x + k + shift) % COLS)
        for k in range(ROWS)
        for x in range(COLS)
    ]


def parts_apart(raw):
    return raw.transpose(1, 0, 2)


def whole(shape):
    return pl.BlockSpec(shape, lambda *_: (0,) * len(shape))


def product(left, right, dim):
    return lax.dot_general(
        left, right, (((1,), (dim,)), ((), ())), preferred_element_type=jnp.float32
    )


def complex_product(lefts, rights, dim, order):
    left = jnp.concatenate([x[...].reshape(-1, x.shape[2]) for x in lefts], axis=1)
    real = jnp.concatenate([rights[e][0] for e in order], axis=dim)
    imag = jnp.concatenate([rights[e][1] for e in order], axis=dim)
    half = left.shape[0] // 2
    u = product(left, real, dim)
    v = product(left, imag, dim)
    return u[:half] - v[half:], u[half:] + v[:half]


def by_atom(re, im):
    rows, columns = re.shape
    pair = [x.reshape(rows // B, B, columns) for x in (re, im)]
    return jnp.stack(pair, axis=1).reshape(2 * rows, columns).astype(jnp.bfloat16)


def coupling_kernel(base_ref, l0, l1, l2, l3, t0, t1, t2, t3, c_ref):
    def run(order):
        re, im = complex_product((l0, l1, l2, l3), (t0, t1, t2, t3), 0, order)
        c_ref[0] = (-re).astype(jnp.bfloat16)
        c_ref[1] = (-im).astype(jnp.bfloat16)

    for base in range(ROWS):

        @pl.when(base_ref[0] == base)
        def _():
            run([(base + d) % ROWS for d in range(ROWS)])


def coupling_call(base, lefts, trails):
    _, rows, inner = lefts[0].shape
    columns = trails[0].shape[2]
    return pl.pallas_call(
        coupling_kernel,
        out_shape=jax.ShapeDtypeStruct((2, rows, columns), jnp.bfloat16),
        grid_spec=pltpu.PrefetchScalarGridSpec(
            num_scalar_prefetch=1,
            grid=(1,),
            in_specs=[whole(lefts[0].shape)] * 4 + [whole(trails[0].shape)] * 4,
            out_specs=whole((2, rows, columns)),
        ),
        compiler_params=pltpu.CompilerParams(vmem_limit_bytes=14 * MIB),
        cost_estimate=pl.CostEstimate(
            flops=2 * rows * inner * 16 * columns, bytes_accessed=3 << 20, transcendentals=0
        ),
        name="coupling",
    )(base, *lefts, *trails)


def take_pairs(codes_ref, counts_ref, mask_ref, pairs_ref, table, lanes, spread, keep, fold):
    owners = pairs_ref.shape[0]

    @pl.loop(0, owners * SLOTS // GROUP)
    def _(group):
        first = group * GROUP
        to = pl.multiple_of(first * 16, GROUP * 16)
        used = counts_ref[first // SLOTS] > first % SLOTS

        @pl.when(used)
        def _():
            for s in range(GROUP):
                code = codes_ref[first + s]
                found = table[pl.ds(pl.multiple_of(code & ~15, 16), 16), :]
                lanes[pl.ds(to + s * 16, 16), :] = found * mask_ref[code & 15]

        @pl.when(jnp.logical_not(used))
        def _():
            lanes[pl.ds(to, GROUP * 16), :] = jnp.zeros((GROUP * 16, 128), jnp.bfloat16)

    many = 4

    @pl.loop(0, owners // many)
    def _(chunk):
        rows = many * SLOTS * 16
        wide = product(lanes[pl.ds(pl.multiple_of(chunk * rows, rows), rows), :], spread[...], 0)
        wide = wide.reshape(many * SLOTS, 2, 8, 2 * B * B) * keep[...][None]
        wide = (wide[:, 0] + wide[:, 1]).reshape(many, SLOTS * 8, 2 * B * B).astype(jnp.bfloat16)
        for o in range(many):
            pairs_ref[chunk * many + o, :SLOTS, :] = product(fold[...], wide[o], 0).astype(
                jnp.bfloat16
            )


def block_kernel(
    base_ref, slot_ref, codes_ref, counts_ref, *refs
):
    first_half, second_half, lowers = refs[:4], refs[4:8], refs[8:12]
    diag_ref, mask_ref, out_ref, pairs_ref, table, lanes, spread, keep, fold = refs[12:]
    step = pl.program_id(0)
    last = pl.num_programs(0) - 1
    tile = out_ref.shape[1]
    per_tile = table.shape[0] // 4
    trail_rows = 2 * refs[0].shape[2]
    super_rows = per_tile - trail_rows

    @pl.when(step == 0)
    def _():
        lane = lax.broadcasted_iota(jnp.int32, (128, 128), 1)
        row = lax.broadcasted_iota(jnp.int32, (128, 128), 0)
        spread[...] = jnp.where(row % 8 == lane % 8, 1.0, 0.0).astype(jnp.bfloat16)
        part = lax.broadcasted_iota(jnp.int32, (2, 8, 128), 0)
        row = lax.broadcasted_iota(jnp.int32, (2, 8, 128), 1)
        lane = lax.broadcasted_iota(jnp.int32, (2, 8, 128), 2)
        keep[...] = jnp.where(lane // 8 == part * 8 + row, 1.0, 0.0)
        row = lax.broadcasted_iota(jnp.int32, fold.shape, 0)
        lane = lax.broadcasted_iota(jnp.int32, fold.shape, 1)
        fold[...] = jnp.where(lane // 8 == row, 1.0, 0.0).astype(jnp.bfloat16)
        slot = jnp.full((8, 128), slot_ref[0], jnp.int32).astype(jnp.float32)
        for owner in range(pairs_ref.shape[0]):
            pairs_ref[owner, SLOTS:, :] = slot.astype(jnp.bfloat16)

    def run(order, couplings):
        re, im = complex_product(couplings, lowers, 1, order)
        re = diag_ref[0].astype(jnp.float32) - re
        im = diag_ref[1].astype(jnp.float32) - im
        out_ref[0] = re.astype(jnp.bfloat16)
        out_ref[1] = im.astype(jnp.bfloat16)
        rows = by_atom(re, im)
        for t in range(4):
            first = pl.multiple_of(t * per_tile + step * 2 * tile, 2 * tile)
            table[pl.ds(first, 2 * tile), :] = rows[:, t * 128 : t * 128 + 128]
        own = [couplings[0][part].astype(jnp.float32).T for part in range(2)]
        rows = by_atom(own[0], own[1])
        for t in range(tile // 128):
            first = pl.multiple_of((step * (tile // 128) + t) * per_tile + super_rows, trail_rows)
            table[pl.ds(first, trail_rows), :] = rows[:, t * 128 : t * 128 + 128]

    for base in range(ROWS):
        for half, couplings in enumerate((first_half, second_half)):

            @pl.when((base_ref[0] == base) & (step == half))
            def _():
                run([(base + d) % ROWS for d in range(ROWS)], couplings)

    @pl.when(step == last)
    def _():
        take_pairs(codes_ref, counts_ref, mask_ref, pairs_ref, table, lanes, spread, keep, fold)


def block_call(base, slot, codes, counts, couplings, lowers, diag, masks):
    _, rows, columns = diag.shape
    inner = couplings[0].shape[2]
    owners = codes.shape[0] // SLOTS
    tile = couplings[0].shape[1]
    row_spec = lambda last: pl.BlockSpec((2, tile, last), lambda i, *_: (0, i, 0))
    return pl.pallas_call(
        block_kernel,
        out_shape=(
            jax.ShapeDtypeStruct((2, rows, columns), jnp.bfloat16),
            jax.ShapeDtypeStruct((owners, SLOTS + 8, 2 * B * B), jnp.bfloat16),
        ),
        grid_spec=pltpu.PrefetchScalarGridSpec(
            num_scalar_prefetch=4,
            grid=(rows // tile,),
            in_specs=[whole(couplings[0].shape)] * 8
            + [whole(lowers[0].shape)] * 4
            + [row_spec(columns), whole(masks.shape)],
            out_specs=(row_spec(columns), whole((owners, SLOTS + 8, 2 * B * B))),
            scratch_shapes=[
                pltpu.VMEM((4 * (2 * rows + 2 * inner), 128), jnp.bfloat16),
                pltpu.VMEM((owners * SLOTS * 16, 128), jnp.bfloat16),
                pltpu.VMEM((128, 128), jnp.bfloat16),
                pltpu.VMEM((2, 8, 128), jnp.float32),
                pltpu.VMEM((SLOTS, SLOTS * 8), jnp.bfloat16),
            ],
        ),
        compiler_params=pltpu.CompilerParams(vmem_limit_bytes=52 * MIB),
        cost_estimate=pl.CostEstimate(
            flops=2 * rows * inner * 16 * columns, bytes_accessed=12 << 20, transcendentals=0
        ),
        name="block_and_pairs",
    )(base, slot, codes, counts, *couplings, *lowers, diag, masks)


def pole_sum_kernel(weight_ref, parts_ref, out_ref):
    lane = lax.broadcasted_iota(jnp.int32, (1, 128), 1).astype(jnp.float32)
    straight = crossed = None
    for p in range(parts_ref.shape[0]):
        part = parts_ref[p, :SLOTS, :].astype(jnp.float32)
        slot = parts_ref[p, SLOTS:, :].astype(jnp.float32)[:1]
        weight = []
        for c in range(2):
            found = jnp.where(slot == lane, weight_ref[c : c + 1, :128], 0.0) + jnp.where(
                slot == lane + 128.0, weight_ref[c : c + 1, 128:], 0.0
            )
            weight.append(jnp.sum(found, axis=1, keepdims=True))
        a = weight[0] * part
        b = weight[1] * part
        straight = a if straight is None else straight + a
        crossed = b if crossed is None else crossed + b
    half = B * B
    lane = lax.broadcasted_iota(jnp.int32, crossed.shape, 1)
    crossed = pltpu.roll(crossed, half, 1)
    total = (straight + jnp.where(lane < half, -crossed, crossed)).astype(out_ref.dtype)
    for cell in range(out_ref.shape[0]):
        out_ref[cell] = total


def pole_sum_call(weights, parts, copies):
    return pl.pallas_call(
        pole_sum_kernel,
        out_shape=jax.ShapeDtypeStruct((copies, SLOTS, 2 * B * B), jnp.bfloat16),
        in_specs=[pl.BlockSpec(memory_space=pltpu.VMEM)] * 2,
        out_specs=pl.BlockSpec(memory_space=pltpu.VMEM),
        compiler_params=pltpu.CompilerParams(vmem_limit_bytes=6 * MIB),
        name="pole_sum",
    )(weights, parts)


def density_kernel(index_ref, sums_ref, projector_ref, out_ref, sums):
    sums[...] = sums_ref[...].astype(jnp.float32)

    @pl.loop(0, out_ref.shape[0] // 32)
    def _(group):
        first = pl.multiple_of(group * 32, 32)
        for s in range(32):
            q = first + s
            out_ref[pl.ds(q, 1), :] = sums[pl.ds(index_ref[q], 1), :]

    out_ref[...] = out_ref[...] * projector_ref[...]


def density_call(index, sums, projector):
    return pl.pallas_call(
        density_kernel,
        out_shape=jax.ShapeDtypeStruct(projector.shape, jnp.float32),
        in_specs=[pl.BlockSpec(memory_space=pltpu.SMEM)]
        + [pl.BlockSpec(memory_space=pltpu.VMEM)] * 2,
        out_specs=pl.BlockSpec(memory_space=pltpu.VMEM),
        scratch_shapes=[pltpu.VMEM(sums.shape, jnp.float32)],
        compiler_params=pltpu.CompilerParams(vmem_limit_bytes=6 * MIB),
        name="density",
    )(index, sums, projector)


def pair_tables(pair_row, pair_col, row, col, pole, owners):
    row_atoms, col_atoms, trail_atoms = KA // ROWS, KA // COLS, 128 // COLS
    a = pair_row.reshape(owners, -1)
    b = pair_col.reshape(owners, -1)
    in_super = a < KA
    trail = a - KA
    cell = jnp.where(
        in_super,
        (a // row_atoms) * COLS + b // col_atoms,
        (b // row_atoms) * COLS + trail // trail_atoms,
    )
    table_atom = jnp.where(in_super, a % row_atoms, row_atoms + trail % trail_atoms)
    column_atom = jnp.where(in_super, b % col_atoms, b % row_atoms)
    tile, place = column_atom // 16, column_atom % 16
    code = (tile * (row_atoms + trail_atoms) + table_atom) * 16 + place
    pairs = a.shape[1]
    place = jnp.arange(pairs, dtype=jnp.int32)
    earlier = place[:, None] < place[None, :]
    mine = cell == row * COLS + col
    rank = jnp.dot(
        mine.astype(jnp.bfloat16),
        earlier.astype(jnp.bfloat16),
        preferred_element_type=jnp.float32,
    ).astype(jnp.int32)
    slot = jnp.where(mine, rank, -1)
    hit = slot[:, None, :] == jnp.arange(SLOTS, dtype=jnp.int32)[None, :, None]
    codes = jnp.sum(jnp.where(hit, code[:, None, :], 0), axis=2).reshape(owners * SLOTS)
    own_cell = lax.dynamic_index_in_dim(cell, pole, 0, keepdims=False)
    same = (own_cell[:, None] == own_cell[None, :]) & earlier
    index = own_cell * SLOTS + jnp.sum(same.astype(jnp.int32), axis=0)
    counts = jnp.sum(mine.astype(jnp.int32), axis=1)
    return codes, counts, index


def local(
    inverse_trail, lower_t, diag_inverse, pole_weight, pole_slot, pair_row, pair_col, projector
):
    row = lax.axis_index("row")
    col = lax.axis_index("col")
    pole = lax.axis_index(POLE)
    poles = lax.axis_size(POLE)
    base = ((row - col + COLS) % COLS).astype(jnp.int32).reshape(1)

    trail = parts_apart(inverse_trail[0])
    lower = parts_apart(lower_t[0])
    half = lower.shape[1] // 2
    halves = [parts_apart(lower_t[0, :half]), parts_apart(lower_t[0, half:])]
    lower, trail, halves = lax.optimization_barrier((lower, trail, halves))
    pair_axes = ("row", "col")

    trails = [trail] + [lax.ppermute(trail, "row", ring(e, ROWS)) for e in range(1, ROWS)]
    first = [lax.ppermute(halves[0], pair_axes, to_process_rows(e)) for e in range(COLS)]
    second_half, _ = lax.optimization_barrier((halves[1], first[0]))
    second = [lax.ppermute(second_half, pair_axes, to_process_rows(e)) for e in range(COLS)]

    codes, counts, index = pair_tables(pair_row, pair_col, row, col, pole, poles)
    diag = parts_apart(diag_inverse[0])
    wide_projector = jnp.concatenate([projector, projector], axis=1).astype(jnp.float32)
    masks = (
        jnp.arange(16, dtype=jnp.int32)[:, None, None]
        == jnp.broadcast_to(jnp.arange(128, dtype=jnp.int32) // B, (16, 128))[None]
    ).astype(jnp.bfloat16)

    trail_base = ((2 * row - col + COLS) % COLS).astype(jnp.int32).reshape(1)
    couplings = []
    for lefts in (first, second):
        coupling = coupling_call(trail_base, lefts, trails)
        if not couplings:
            lower_late, coupling = lax.optimization_barrier((lower, coupling))
        couplings += [coupling] + [
            lax.ppermute(coupling, "col", ring(d, COLS)) for d in range(1, COLS)
        ]
    lower_early, _ = lax.optimization_barrier((lower, second[1]))
    lowers = [lower] + [
        lax.ppermute(lower_early if e == 2 else lower_late, "row", ring(e, ROWS))
        for e in range(1, ROWS)
    ]

    block, pairs = block_call(
        base, pole_slot, codes, counts, couplings, lowers, diag, masks
    )
    out = block.transpose(1, 0, 2)[None]

    parts = lax.all_to_all(pairs, POLE, 0, 0, tiled=True)
    cells = ROWS * COLS
    summed = pole_sum_call(pole_weight.T, parts, cells)
    everywhere = lax.all_to_all(summed, ("row", "col"), 0, 0, tiled=True)
    density = density_call(index, everywhere.reshape(cells * SLOTS, 2 * B * B), wide_projector)
    return (out, density)


def solution(mesh):
    split = Mesh(
        mesh.devices.reshape(8, 2, mesh.shape["row"], mesh.shape["col"]),
        ("pole_0", "pole_1", "row", "col"),
    )
    in_specs = (
        P(POLE, "row", None, "col"),
        P(POLE, "col", None, "row"),
        P(POLE, "row", None, "col"),
        P(),
        P(POLE),
        P(),
        P(),
        P(POLE, None),
    )
    out_specs = (P(POLE, "row", None, "col"), P(POLE, None))
    return jax.shard_map(local, mesh=split, in_specs=in_specs, out_specs=out_specs, check_vma=False)
```

```python
import jax
import jax.numpy as jnp
from jax import lax
from jax.experimental import pallas as pl
from jax.experimental.pallas import tpu as pltpu
from jax.sharding import Mesh
from jax.sharding import PartitionSpec as P

B = 8
KA = 256
POLE = ("pole_0", "pole_1")
ROWS = 4
COLS = 4
SLOTS = 64
GROUP = 16
MIB = 1 << 20


def ring(shift, peers):
    return [(i, (i + shift) % peers) for i in range(peers)]


def to_process_rows(shift):
    return [
        (k * COLS + x, x * COLS + (x + k + shift) % COLS)
        for k in range(ROWS)
        for x in range(COLS)
    ]


def parts_apart(raw):
    return raw.transpose(1, 0, 2)


def whole(shape):
    return pl.BlockSpec(shape, lambda *_: (0,) * len(shape))


def product(left, right, dim):
    return lax.dot_general(
        left, right, (((1,), (dim,)), ((), ())), preferred_element_type=jnp.float32
    )


def complex_product(lefts, rights, dim, order):
    left = jnp.concatenate([x[...].reshape(-1, x.shape[2]) for x in lefts], axis=1)
    real = jnp.concatenate([rights[e][0] for e in order], axis=dim)
    imag = jnp.concatenate([rights[e][1] for e in order], axis=dim)
    half = left.shape[0] // 2
    u = product(left, real, dim)
    v = product(left, imag, dim)
    return u[:half] - v[half:], u[half:] + v[:half]


def by_atom(re, im):
    rows, columns = re.shape
    pair = [x.reshape(rows // B, B, columns) for x in (re, im)]
    return jnp.stack(pair, axis=1).reshape(2 * rows, columns).astype(jnp.bfloat16)


def coupling_kernel(base_ref, l0, l1, l2, l3, t0, t1, t2, t3, c_ref):
    def run(order):
        re, im = complex_product((l0, l1, l2, l3), (t0, t1, t2, t3), 0, order)
        c_ref[0] = (-re).astype(jnp.bfloat16)
        c_ref[1] = (-im).astype(jnp.bfloat16)

    for base in range(ROWS):

        @pl.when(base_ref[0] == base)
        def _():
            run([(base + d) % ROWS for d in range(ROWS)])


def coupling_call(base, lefts, trails):
    _, rows, inner = lefts[0].shape
    columns = trails[0].shape[2]
    return pl.pallas_call(
        coupling_kernel,
        out_shape=jax.ShapeDtypeStruct((2, rows, columns), jnp.bfloat16),
        grid_spec=pltpu.PrefetchScalarGridSpec(
            num_scalar_prefetch=1,
            grid=(1,),
            in_specs=[whole(lefts[0].shape)] * 4 + [whole(trails[0].shape)] * 4,
            out_specs=whole((2, rows, columns)),
        ),
        compiler_params=pltpu.CompilerParams(vmem_limit_bytes=14 * MIB),
        cost_estimate=pl.CostEstimate(
            flops=2 * rows * inner * 16 * columns, bytes_accessed=3 << 20, transcendentals=0
        ),
        name="coupling",
    )(base, *lefts, *trails)


def take_pairs(codes_ref, counts_ref, mask_ref, pairs_ref, table, lanes, spread, keep, fold):
    owners = pairs_ref.shape[0]

    @pl.loop(0, owners * SLOTS // GROUP)
    def _(group):
        first = group * GROUP
        to = pl.multiple_of(first * 16, GROUP * 16)
        used = counts_ref[first // SLOTS] > first % SLOTS

        @pl.when(used)
        def _():
            for s in range(GROUP):
                code = codes_ref[first + s]
                found = table[pl.ds(pl.multiple_of(code & ~15, 16), 16), :]
                lanes[pl.ds(to + s * 16, 16), :] = found * mask_ref[code & 15]

        @pl.when(jnp.logical_not(used))
        def _():
            lanes[pl.ds(to, GROUP * 16), :] = jnp.zeros((GROUP * 16, 128), jnp.bfloat16)

    many = 4

    @pl.loop(0, owners // many)
    def _(chunk):
        rows = many * SLOTS * 16
        wide = product(lanes[pl.ds(pl.multiple_of(chunk * rows, rows), rows), :], spread[...], 0)
        wide = wide.reshape(many * SLOTS, 2, 8, 2 * B * B) * keep[...][None]
        wide = (wide[:, 0] + wide[:, 1]).reshape(many, SLOTS * 8, 2 * B * B).astype(jnp.bfloat16)
        for o in range(many):
            pairs_ref[chunk * many + o, :SLOTS, :] = product(fold[...], wide[o], 0).astype(
                jnp.bfloat16
            )


def block_kernel(
    base_ref, slot_ref, codes_ref, counts_ref, *refs
):
    first_half, second_half, lowers = refs[:4], refs[4:8], refs[8:12]
    diag_ref, mask_ref, out_ref, pairs_ref, table, lanes, spread, keep, fold = refs[12:]
    step = pl.program_id(0)
    last = pl.num_programs(0) - 1
    tile = out_ref.shape[1]
    per_tile = table.shape[0] // 4
    trail_rows = 2 * refs[0].shape[2]
    super_rows = per_tile - trail_rows

    @pl.when(step == 0)
    def _():
        lane = lax.broadcasted_iota(jnp.int32, (128, 128), 1)
        row = lax.broadcasted_iota(jnp.int32, (128, 128), 0)
        spread[...] = jnp.where(row % 8 == lane % 8, 1.0, 0.0).astype(jnp.bfloat16)
        part = lax.broadcasted_iota(jnp.int32, (2, 8, 128), 0)
        row = lax.broadcasted_iota(jnp.int32, (2, 8, 128), 1)
        lane = lax.broadcasted_iota(jnp.int32, (2, 8, 128), 2)
        keep[...] = jnp.where(lane // 8 == part * 8 + row, 1.0, 0.0)
        row = lax.broadcasted_iota(jnp.int32, fold.shape, 0)
        lane = lax.broadcasted_iota(jnp.int32, fold.shape, 1)
        fold[...] = jnp.where(lane // 8 == row, 1.0, 0.0).astype(jnp.bfloat16)
        slot = jnp.full((8, 128), slot_ref[0], jnp.int32).astype(jnp.float32)
        for owner in range(pairs_ref.shape[0]):
            pairs_ref[owner, SLOTS:, :] = slot.astype(jnp.bfloat16)

    def run(order, couplings):
        re, im = complex_product(couplings, lowers, 1, order)
        re = diag_ref[0].astype(jnp.float32) - re
        im = diag_ref[1].astype(jnp.float32) - im
        out_ref[0] = re.astype(jnp.bfloat16)
        out_ref[1] = im.astype(jnp.bfloat16)
        rows = by_atom(re, im)
        for t in range(4):
            first = pl.multiple_of(t * per_tile + step * 2 * tile, 2 * tile)
            table[pl.ds(first, 2 * tile), :] = rows[:, t * 128 : t * 128 + 128]
        own = [couplings[0][part].astype(jnp.float32).T for part in range(2)]
        rows = by_atom(own[0], own[1])
        for t in range(tile // 128):
            first = pl.multiple_of((step * (tile // 128) + t) * per_tile + super_rows, trail_rows)
            table[pl.ds(first, trail_rows), :] = rows[:, t * 128 : t * 128 + 128]

    for base in range(ROWS):
        for half, couplings in enumerate((first_half, second_half)):

            @pl.when((base_ref[0] == base) & (step == half))
            def _():
                run([(base + d) % ROWS for d in range(ROWS)], couplings)

    @pl.when(step == last)
    def _():
        take_pairs(codes_ref, counts_ref, mask_ref, pairs_ref, table, lanes, spread, keep, fold)


def block_call(base, slot, codes, counts, couplings, lowers, diag, masks):
    _, rows, columns = diag.shape
    inner = couplings[0].shape[2]
    owners = codes.shape[0] // SLOTS
    tile = couplings[0].shape[1]
    row_spec = lambda last: pl.BlockSpec((2, tile, last), lambda i, *_: (0, i, 0))
    return pl.pallas_call(
        block_kernel,
        out_shape=(
            jax.ShapeDtypeStruct((2, rows, columns), jnp.bfloat16),
            jax.ShapeDtypeStruct((owners, SLOTS + 8, 2 * B * B), jnp.bfloat16),
        ),
        grid_spec=pltpu.PrefetchScalarGridSpec(
            num_scalar_prefetch=4,
            grid=(rows // tile,),
            in_specs=[whole(couplings[0].shape)] * 8
            + [whole(lowers[0].shape)] * 4
            + [row_spec(columns), whole(masks.shape)],
            out_specs=(row_spec(columns), whole((owners, SLOTS + 8, 2 * B * B))),
            scratch_shapes=[
                pltpu.VMEM((4 * (2 * rows + 2 * inner), 128), jnp.bfloat16),
                pltpu.VMEM((owners * SLOTS * 16, 128), jnp.bfloat16),
                pltpu.VMEM((128, 128), jnp.bfloat16),
                pltpu.VMEM((2, 8, 128), jnp.float32),
                pltpu.VMEM((SLOTS, SLOTS * 8), jnp.bfloat16),
            ],
        ),
        compiler_params=pltpu.CompilerParams(vmem_limit_bytes=52 * MIB),
        cost_estimate=pl.CostEstimate(
            flops=2 * rows * inner * 16 * columns, bytes_accessed=12 << 20, transcendentals=0
        ),
        name="block_and_pairs",
    )(base, slot, codes, counts, *couplings, *lowers, diag, masks)


def pole_sum_kernel(weight_ref, parts_ref, out_ref):
    lane = lax.broadcasted_iota(jnp.int32, (1, 128), 1).astype(jnp.float32)
    straight = crossed = None
    for p in range(parts_ref.shape[0]):
        part = parts_ref[p, :SLOTS, :].astype(jnp.float32)
        slot = parts_ref[p, SLOTS:, :].astype(jnp.float32)[:1]
        weight = []
        for c in range(2):
            found = jnp.where(slot == lane, weight_ref[c : c + 1, :128], 0.0) + jnp.where(
                slot == lane + 128.0, weight_ref[c : c + 1, 128:], 0.0
            )
            weight.append(jnp.sum(found, axis=1, keepdims=True))
        a = weight[0] * part
        b = weight[1] * part
        straight = a if straight is None else straight + a
        crossed = b if crossed is None else crossed + b
    half = B * B
    lane = lax.broadcasted_iota(jnp.int32, crossed.shape, 1)
    crossed = pltpu.roll(crossed, half, 1)
    total = (straight + jnp.where(lane < half, -crossed, crossed)).astype(out_ref.dtype)
    for cell in range(out_ref.shape[0]):
        out_ref[cell] = total


def pole_sum_call(weights, parts, copies):
    return pl.pallas_call(
        pole_sum_kernel,
        out_shape=jax.ShapeDtypeStruct((copies, SLOTS, 2 * B * B), jnp.bfloat16),
        in_specs=[pl.BlockSpec(memory_space=pltpu.VMEM)] * 2,
        out_specs=pl.BlockSpec(memory_space=pltpu.VMEM),
        compiler_params=pltpu.CompilerParams(vmem_limit_bytes=6 * MIB),
        name="pole_sum",
    )(weights, parts)


def density_kernel(index_ref, sums_ref, projector_ref, out_ref, sums):
    sums[...] = sums_ref[...].astype(jnp.float32)

    @pl.loop(0, out_ref.shape[0] // 32)
    def _(group):
        first = pl.multiple_of(group * 32, 32)
        for s in range(32):
            q = first + s
            out_ref[pl.ds(q, 1), :] = sums[pl.ds(index_ref[q], 1), :]

    out_ref[...] = out_ref[...] * projector_ref[...]


def density_call(index, sums, projector):
    return pl.pallas_call(
        density_kernel,
        out_shape=jax.ShapeDtypeStruct(projector.shape, jnp.float32),
        in_specs=[pl.BlockSpec(memory_space=pltpu.SMEM)]
        + [pl.BlockSpec(memory_space=pltpu.VMEM)] * 2,
        out_specs=pl.BlockSpec(memory_space=pltpu.VMEM),
        scratch_shapes=[pltpu.VMEM(sums.shape, jnp.float32)],
        compiler_params=pltpu.CompilerParams(vmem_limit_bytes=6 * MIB),
        name="density",
    )(index, sums, projector)


def pair_tables(pair_row, pair_col, row, col, pole, owners):
    row_atoms, col_atoms, trail_atoms = KA // ROWS, KA // COLS, 128 // COLS
    a = pair_row.reshape(owners, -1)
    b = pair_col.reshape(owners, -1)
    in_super = a < KA
    trail = a - KA
    cell = jnp.where(
        in_super,
        (a // row_atoms) * COLS + b // col_atoms,
        (b // row_atoms) * COLS + trail // trail_atoms,
    )
    table_atom = jnp.where(in_super, a % row_atoms, row_atoms + trail % trail_atoms)
    column_atom = jnp.where(in_super, b % col_atoms, b % row_atoms)
    tile, place = column_atom // 16, column_atom % 16
    code = (tile * (row_atoms + trail_atoms) + table_atom) * 16 + place
    pairs = a.shape[1]
    place = jnp.arange(pairs, dtype=jnp.int32)
    earlier = place[:, None] < place[None, :]
    mine = cell == row * COLS + col
    rank = jnp.dot(
        mine.astype(jnp.bfloat16),
        earlier.astype(jnp.bfloat16),
        preferred_element_type=jnp.float32,
    ).astype(jnp.int32)
    slot = jnp.where(mine, rank, -1)
    hit = slot[:, None, :] == jnp.arange(SLOTS, dtype=jnp.int32)[None, :, None]
    codes = jnp.sum(jnp.where(hit, code[:, None, :], 0), axis=2).reshape(owners * SLOTS)
    own_cell = lax.dynamic_index_in_dim(cell, pole, 0, keepdims=False)
    same = (own_cell[:, None] == own_cell[None, :]) & earlier
    index = own_cell * SLOTS + jnp.sum(same.astype(jnp.int32), axis=0)
    counts = jnp.sum(mine.astype(jnp.int32), axis=1)
    return codes, counts, index


def local(
    inverse_trail, lower_t, diag_inverse, pole_weight, pole_slot, pair_row, pair_col, projector
):
    row = lax.axis_index("row")
    col = lax.axis_index("col")
    pole = lax.axis_index(POLE)
    poles = lax.axis_size(POLE)
    base = ((row - col + COLS) % COLS).astype(jnp.int32).reshape(1)

    trail = parts_apart(inverse_trail[0])
    lower = parts_apart(lower_t[0])
    half = lower.shape[1] // 2
    halves = [parts_apart(lower_t[0, :half]), parts_apart(lower_t[0, half:])]
    lower, trail, halves = lax.optimization_barrier((lower, trail, halves))
    pair_axes = ("row", "col")

    trails = [trail] + [lax.ppermute(trail, "row", ring(e, ROWS)) for e in range(1, ROWS)]
    first = [lax.ppermute(halves[0], pair_axes, to_process_rows(e)) for e in range(COLS)]
    second_half, _ = lax.optimization_barrier((halves[1], first[0]))
    second = [lax.ppermute(second_half, pair_axes, to_process_rows(e)) for e in range(COLS)]

    codes, counts, index = pair_tables(pair_row, pair_col, row, col, pole, poles)
    diag = parts_apart(diag_inverse[0])
    wide_projector = jnp.concatenate([projector, projector], axis=1).astype(jnp.float32)
    masks = (
        jnp.arange(16, dtype=jnp.int32)[:, None, None]
        == jnp.broadcast_to(jnp.arange(128, dtype=jnp.int32) // B, (16, 128))[None]
    ).astype(jnp.bfloat16)

    trail_base = ((2 * row - col + COLS) % COLS).astype(jnp.int32).reshape(1)
    couplings = []
    for lefts in (first, second):
        coupling = coupling_call(trail_base, lefts, trails)
        if not couplings:
            lower_late, coupling = lax.optimization_barrier((lower, coupling))
        couplings += [coupling] + [
            lax.ppermute(coupling, "col", ring(d, COLS)) for d in range(1, COLS)
        ]
    lower_early, _ = lax.optimization_barrier((lower, second[1]))
    lowers = [lower] + [
        lax.ppermute(lower_early if e == 1 else lower_late, "row", ring(e, ROWS))
        for e in range(1, ROWS)
    ]

    block, pairs = block_call(
        base, pole_slot, codes, counts, couplings, lowers, diag, masks
    )
    out = block.transpose(1, 0, 2)[None]

    parts = lax.all_to_all(pairs, POLE, 0, 0, tiled=True)
    cells = ROWS * COLS
    summed = pole_sum_call(pole_weight.T, parts, cells)
    everywhere = lax.all_to_all(summed, ("row", "col"), 0, 0, tiled=True)
    density = density_call(index, everywhere.reshape(cells * SLOTS, 2 * B * B), wide_projector)
    return (out, density)


def solution(mesh):
    split = Mesh(
        mesh.devices.reshape(8, 2, mesh.shape["row"], mesh.shape["col"]),
        ("pole_0", "pole_1", "row", "col"),
    )
    in_specs = (
        P(POLE, "row", None, "col"),
        P(POLE, "col", None, "row"),
        P(POLE, "row", None, "col"),
        P(),
        P(POLE),
        P(),
        P(),
        P(POLE, None),
    )
    out_specs = (P(POLE, "row", None, "col"), P(POLE, None))
    return jax.shard_map(local, mesh=split, in_specs=in_specs, out_specs=out_specs, check_vma=False)
```
